512 devices in a mesh: grp: 16 (over y, core), dev: 32 (over z, x).
Axes of the slice: x: 4, y: 8, z: 8, core: 2. Of those that a mesh axis runs over, the one named last changes fastest.
Arguments:
- basis_values: bfloat16 [2048, 256, 512], P(('grp', 'dev')), may hold values from -1 to 1
- stored_density_blocks: bfloat16 [256, 128, 128], P('dev'), may hold values from -0.5 to 0.5
- device_request: int32 [512, 32, 2], P(('grp', 'dev')), may hold values from -1 to 7, as said below
- batch_blocks: int32 [2048, 16], P(('grp', 'dev')), may hold values from 0 to 63, as said below
- batch_atom: int32 [2048], P(('grp', 'dev')), may hold values from 0 to 999
- point_offset: float32 [3, 2048, 256], P(None, ('grp', 'dev')), may hold values from -8 to 8
- point_weight: float32 [2048, 256], P(('grp', 'dev')), may hold values from 0.02 to 0.5
- exchange_kernel: float32 [2048, 256], P(('grp', 'dev')), may hold values from -3 to -0.3
- atom_xyz: float32 [3, 1000], replicated, may hold values from -15 to 15
Outputs:
- response_hamiltonian: bfloat16 [256, 128, 128], P('dev')
- response_density: float32 [2048, 256], P(('grp', 'dev'))
- multipoles: float32 [4, 1000], replicated
The draws below stay inside these ranges and needn't reach their ends.
Inputs may be any that keep to these rules, and one draw needn't show every extreme that they name: `device_request`: row d belongs to device d of grp+dev in grp-major order. Each row has exactly 32 entries other than -1, distinct for one owner; in every group one owner is asked for 2 blocks by every device of the group. `batch_blocks`: every entry points to an entry of its device's request row that is not -1.
All inputs are finite; a program needn't handle non-finite values.
Results may differ from the reference program's by a relative error of at most 0.004.
Values may be sent and summed in bfloat16 or wider, within the bound.
No kernel may reach another device: no remote copies, remote signals or barrier semaphores. Data moves between devices by JAX's collectives and lax.ppermute only.
A program may use at most 64 MiB of HBM per device.

```python
import math
import jax
import jax.numpy as jnp
from jax import lax

TILE_FUNCTIONS = 128
REL = 4
PTS = 256
BATCH_DEV = 4
OWN_DEV = 8
NEED = 32
ATOMS = 1000
OWNERS = 32
CAP = 2
NBATCH = 2048
STORED_BLOCKS = 256


def request_layout(key):
    device_list = NBATCH // BATCH_DEV
    positions = OWNERS * CAP
    hot = jax.random.randint(jax.random.fold_in(key, 11), (device_list // OWNERS,), 0, OWNERS)
    hot_device = jnp.repeat(hot, OWNERS)
    owner_of = jnp.arange(positions, dtype=jnp.int32) // CAP
    noise = jax.random.randint(jax.random.fold_in(key, 12), (device_list, positions), 1, 2 ** 20)
    index = jnp.arange(positions, dtype=jnp.int32)[None, :]
    score = jnp.where(owner_of[None, :] == hot_device[:, None], index, noise * positions + index)
    order = jnp.argsort(score, axis=1).astype(jnp.int32)
    rank = jnp.argsort(order, axis=1)
    live = rank < NEED
    shuffle = jax.random.randint(jax.random.fold_in(key, 13), (device_list, OWNERS, OWN_DEV), 0, 2 ** 20)
    rank_ordered = shuffle * OWN_DEV + jnp.arange(OWN_DEV, dtype=jnp.int32)
    picks = jnp.argsort(rank_ordered, axis=2)[:, :, :CAP].astype(jnp.int32)
    request = jnp.where(live.reshape(device_list, OWNERS, CAP), picks, -1).astype(jnp.int32)
    return (request, order[:, :NEED])


def draw_device_request(key, part):
    return request_layout(key)[0]


def draw_batch_blocks(key, part):
    request, live_positions = request_layout(key)
    device_list = NBATCH // BATCH_DEV
    chosen = jax.random.randint(jax.random.fold_in(key, 14), (device_list, BATCH_DEV * REL * REL), 0, NEED)
    picked = jnp.take_along_axis(live_positions, chosen, axis=1)
    return picked.reshape(NBATCH, REL * REL).astype(jnp.int32)


def with_ends(values, rng, smallest, high):
    index_at = [jax.random.randint(jax.random.fold_in(rng, axis), (), 0, length) for axis, length in enumerate(values.shape)]
    widest = values.shape.index(max(values.shape))
    next_to = index_at[:widest] + [(index_at[widest] + 1) % values.shape[widest]] + index_at[widest + 1:]
    return values.at[tuple(index_at)].set(smallest).at[tuple(next_to)].set(high)


def shard_levels(rng, extent, cuts, smallest, top_value):
    level, own = 1.0, jax.random.fold_in(rng, 6)
    for position, blocks in cuts:
        steps = jnp.exp(jax.random.uniform(jax.random.fold_in(own, position), (blocks,), jnp.float32, smallest / len(cuts), top_value / len(cuts)))
        level = level * jnp.repeat(steps, extent[position] // blocks).reshape([-1 if axis == position else 1 for axis in range(len(extent))])
    return level


def scatter_about(stream_key, dims, deviation, reach, pieces=(), kind=jnp.bfloat16):
    array = deviation * jax.random.normal(stream_key, dims, jnp.float32)
    if pieces:
        array = array * shard_levels(stream_key, dims, pieces, -0.22, 0.18)
    return jnp.clip(array, -reach, reach).astype(kind)


def setup_inputs(seed: int = 0) -> dict:
    keys = jax.random.split(jax.random.key(seed), 10)
    basis_values = scatter_about(keys[0], (NBATCH, PTS, REL * TILE_FUNCTIONS), 0.15, 1.0, ((0, 512),))
    stored_density_blocks = scatter_about(keys[1], (STORED_BLOCKS, TILE_FUNCTIONS, TILE_FUNCTIONS), TILE_FUNCTIONS ** -0.5, 0.5, ((0, 32),))
    device_request = draw_device_request(jax.random.fold_in(keys[9], 71), 0)
    batch_blocks = draw_batch_blocks(jax.random.fold_in(keys[9], 71), 0)
    batch_atom = with_ends(jax.random.randint(keys[4], (NBATCH,), 0, ATOMS), jax.random.fold_in(keys[4], 1), 0, ATOMS - 1).astype(jnp.int32)
    point_offset = scatter_about(keys[5], (3, NBATCH, PTS), 1.5, 8.0, ((1, 512),), jnp.float32)
    point_weight = jnp.clip(jnp.exp(math.log(0.5) - 3.218876 * jax.random.uniform(keys[6], (NBATCH, PTS), jnp.float32) ** shard_levels(keys[6], (NBATCH, PTS), ((0, 512),), -0.2, 0.2)), 0.02, 0.5)
    exchange_kernel = jnp.clip(-3.0 + 2.7 * jax.random.uniform(keys[7], (NBATCH, PTS), jnp.float32) ** shard_levels(keys[7], (NBATCH, PTS), ((0, 512),), -0.2, 0.2), -3.0, -0.3)
    atom_xyz = jnp.clip(jax.random.uniform(keys[8], (3, ATOMS), jnp.float32, -15.0, 15.0), -15.0, 15.0)
    return {"basis_values": basis_values, "stored_density_blocks": stored_density_blocks, "device_request": device_request, "batch_blocks": batch_blocks, "batch_atom": batch_atom, "point_offset": point_offset, "point_weight": point_weight, "exchange_kernel": exchange_kernel, "atom_xyz": atom_xyz}


HIGH = lax.Precision.HIGHEST

def far_field(multipoles, centre, offset, atom_xyz):
    gap = centre[:, None, None] + offset[:, :, None] - atom_xyz[:, None, :]
    inverse = lax.rsqrt(gap[0] * gap[0] + gap[1] * gap[1] + gap[2] * gap[2] + 1.0)
    cube = inverse * inverse * inverse
    dipole = multipoles[1] * gap[0] + multipoles[2] * gap[1] + multipoles[3] * gap[2]
    return lax.optimization_barrier(jnp.sum(multipoles[0] * inverse + dipole * cube, axis=1))

def reference(basis_values, stored_density_blocks, device_request, batch_blocks, batch_atom, point_offset, point_weight, exchange_kernel, atom_xyz):
    device_list, owners, capacity = device_request.shape
    own = stored_density_blocks.shape[0] // owners
    tile = stored_density_blocks.shape[1]
    batches, points, width = basis_values.shape
    rel = width // tile
    per_dev = batches // device_list
    atoms = atom_xyz.shape[1]
    owner_base = (jnp.arange(owners, dtype=jnp.int32) * own)[None, :, None]
    wanted = jnp.where(device_request >= 0, device_request + owner_base, -1).reshape(device_list, owners * capacity)
    batch_home = (jnp.arange(batches, dtype=jnp.int32) // per_dev).astype(jnp.int32)
    batch_slots = jnp.take_along_axis(wanted[batch_home], batch_blocks, axis=1)

    def density_one(args):
        values, slots = args
        blocks = stored_density_blocks[slots].astype(jnp.float32).reshape(rel, rel, tile, tile)
        split = values.astype(jnp.float32).reshape(points, rel, tile)
        left = jnp.einsum('rim,ijmn->rijn', split, blocks)
        return jnp.einsum('rijn,rjn->r', left, split)
    density_field = lax.map(density_one, (basis_values, batch_slots))
    weighted = density_field * point_weight
    parts = jnp.stack([lax.optimization_barrier(jnp.sum(weighted, 1)), lax.optimization_barrier(jnp.sum(weighted * point_offset[0], 1)), lax.optimization_barrier(jnp.sum(weighted * point_offset[1], 1)), lax.optimization_barrier(jnp.sum(weighted * point_offset[2], 1))])
    onehot = (batch_atom[:, None] == jnp.arange(atoms, dtype=jnp.int32)[None, :]).astype(jnp.float32)
    multipoles = jnp.dot(parts, onehot, precision=HIGH)
    centres = jnp.take(atom_xyz, batch_atom, axis=1)

    def potential_one(args):
        centre, offset = args
        return far_field(multipoles, centre, offset, atom_xyz)
    hartree = lax.map(potential_one, (centres.T, jnp.moveaxis(point_offset, 1, 0)))
    xc_part = point_weight * exchange_kernel * density_field
    hartree_part = point_weight * hartree

    def pair_terms(args):
        values, first, second = args
        wide = values.astype(jnp.float32)
        split = wide.reshape(points, rel, tile)
        one = (wide * first[:, None]).astype(jnp.bfloat16).astype(jnp.float32).reshape(points, rel, tile)
        two = (wide * second[:, None]).astype(jnp.bfloat16).astype(jnp.float32).reshape(points, rel, tile)
        return jnp.einsum('rim,rjn->ijmn', one, split) + jnp.einsum('rim,rjn->ijmn', two, split)

    def per_device(total, args):
        values, first, second, positions, requested_row = args
        terms = lax.map(pair_terms, (values, first, second))
        summed = jax.ops.segment_sum(terms.reshape(per_dev * rel * rel, tile * tile), positions.reshape(-1), num_segments=owners * capacity)
        rounded = lax.optimization_barrier(summed.astype(jnp.bfloat16)).astype(jnp.float32)
        target = jnp.where(requested_row >= 0, requested_row, total.shape[0]).astype(jnp.int32)
        return (total.at[target].add(rounded, mode='drop'), None)
    start_total = jnp.zeros((owners * own, tile * tile), jnp.float32)
    total, _ = lax.scan(per_device, start_total, (basis_values.reshape(device_list, per_dev, points, width), xc_part.reshape(device_list, per_dev, points), hartree_part.reshape(device_list, per_dev, points), batch_blocks.reshape(device_list, per_dev, rel * rel), wanted))
    hamiltonian = total.astype(jnp.bfloat16).reshape(owners * own, tile, tile)
    return (hamiltonian, density_field, multipoles)
```

```python
import functools

import jax
import jax.numpy as jnp
from jax import lax
from jax.experimental import pallas as pl
from jax.experimental.pallas import tpu as pltpu
from jax.sharding import Mesh
from jax.sharding import PartitionSpec as P

GRP = ("y4", "y2", "c")
DEV = ("z4", "z2", "x")
GRP_DEV = GRP + DEV
SERVE = ("c", "z2", "x")
COLLECT = ("y2", "c", "z2", "x")
SETTLE = ("y4", "z4")

F32 = jnp.float32
BF16 = jnp.bfloat16
MIB = 1024 * 1024
VALUES = 8


def exchange(value, axes):
    return lax.all_to_all(value, axes, split_axis=0, concat_axis=0, tiled=True)


def vmem(count):
    return [pl.BlockSpec(memory_space=pltpu.VMEM)] * count


def smem(count):
    return [pl.BlockSpec(memory_space=pltpu.SMEM)] * count


def place_of(position):
    return (position >> 1) & 7, (position >> 4) * 2 + (position & 1)


def serve_kernel(ids, z4, own, one, two, three, out, held):
    for shift, piece in enumerate((own, one, two, three)):
        held[(z4[0] - shift) & 3] = piece[...]

    def serve_one(n, _):
        for k in range(8):
            block = jnp.maximum(ids[n * 8 + k], 0)
            out[n, k] = held[k // 2, block]
        return 0

    lax.fori_loop(0, out.shape[0], serve_one, 0)


def density_kernel(needed, atom, phi, blocks, weight, offset, rho_out, share_out, wide):
    batches, points, width = phi.shape
    rel = width // 128
    half = blocks.shape[2]
    lane = lax.broadcasted_iota(jnp.int32, (points, 128), 1)
    columns = jnp.zeros((points, 128), F32)
    for b in range(batches):
        for p in range(rel * rel):
            w, k = place_of(needed[b * rel * rel + p])
            i, j = p // rel, p % rel
            for c in range(2):
                wide[b % 2, pl.ds(i * 128 + c * half, half), pl.ds(j * 128, 128)] = blocks[c * 8 + w, k]
        values = phi[b]
        product = jnp.dot(values, wide[b % 2], preferred_element_type=F32) * values.astype(F32)
        folded = product[:, :128]
        for j in range(1, rel):
            folded = folded + product[:, j * 128 : (j + 1) * 128]
        columns = jnp.where(lane == b, jnp.sum(folded, axis=1, keepdims=True), columns)
    rho = columns.T[:batches]
    rho_out[...] = rho
    weighted = rho * weight[...]
    moments = [weighted] + [weighted * offset[k] for k in range(3)]
    spot = lax.broadcasted_iota(jnp.int32, (batches, 128), 1)
    row = lax.broadcasted_iota(jnp.int32, (batches, 128), 0)
    tile = jnp.zeros((batches, 128), F32)
    for k, moment in enumerate(moments):
        tile = jnp.where(spot % VALUES == k, jnp.sum(moment, axis=1, keepdims=True), tile)
    for b in range(batches):
        tile = jnp.where((spot % VALUES == 4) & (row == b), atom[b].astype(F32), tile)
    tile = jnp.where(spot // VALUES == row, tile, 0.0)
    flat = jnp.sum(tile, axis=0, keepdims=True)[:, : batches * VALUES]
    share_out[...] = jnp.broadcast_to(flat, share_out.shape)


def term_kernel(
    needed,
    atom,
    places,
    shares,
    phi,
    rho,
    weight,
    exchange_part,
    offset,
    xyz,
    multipoles_out,
    out,
    rows,
    spread,
    points_at,
    potential,
    total,
):
    batches, points, width = phi.shape
    rel = width // 128
    devices, lanes = rows.shape
    group = devices // shares.shape[0]
    each = batches * VALUES
    atoms = xyz.shape[1]

    rows[...] = jnp.zeros_like(rows)
    for g in range(group):
        rows[g * shares.shape[0] : (g + 1) * shares.shape[0], :each] = shares[:, g * each : (g + 1) * each]
    table = rows[...]
    turned = table.T
    atom_at = lax.broadcasted_iota(jnp.int32, (devices, atoms), 1).astype(F32)
    summed = jnp.zeros((VALUES * 3, atoms), F32)
    for b in range(batches):
        member = table[:, b * VALUES + 4 : b * VALUES + 5] == atom_at
        member = jnp.where(member, 1.0, 0.0).astype(BF16)
        exact = turned[b * VALUES : (b + 1) * VALUES]
        high = exact.astype(BF16)
        rest = exact - high.astype(F32)
        middle = rest.astype(BF16)
        low = (rest - middle.astype(F32)).astype(BF16)
        three = jnp.concatenate([high.astype(F32), middle.astype(F32), low.astype(F32)], axis=0)
        summed = summed + jnp.dot(three.astype(BF16), member, preferred_element_type=F32)
    multipoles = summed[:VALUES] + (summed[VALUES : 2 * VALUES] + summed[2 * VALUES :])
    multipoles_out[...] = multipoles

    chunks = atoms // 128
    for h in range(chunks):
        at = slice(h * 128, (h + 1) * 128)
        for k in range(3):
            spread[k * chunks + h] = jnp.broadcast_to(xyz[k : k + 1, at], (8, 128))
        for k in range(4):
            spread[(3 + k) * chunks + h] = jnp.broadcast_to(multipoles[k : k + 1, at], (8, 128))

    rho_now = rho[...]
    filler = jnp.zeros((128 - 6 * batches, points), F32)
    features = jnp.concatenate(
        [weight[...], exchange_part[...] * rho_now, offset[0], offset[1], offset[2], rho_now, filler], axis=0
    )
    features = features.T
    for b in range(batches):
        for k in range(3):
            at = (2 + k) * batches + b
            spot = features[:, at : at + 1] + places[k, atom[b]]
            points_at[k, b * points // 8 : (b + 1) * points // 8] = jnp.broadcast_to(
                spot, (points, 128)
            ).reshape(points // 8, 8, 128)

    def potential_of(step, _):
        at = pl.ds(step * 8, 8)
        px, py, pz = points_at[0, at], points_at[1, at], points_at[2, at]
        acc = jnp.zeros((8, 8, 128), F32)
        for h in range(chunks):
            gx = px - spread[h][None]
            gy = py - spread[chunks + h][None]
            gz = pz - spread[2 * chunks + h][None]
            inverse = lax.rsqrt(gx * gx + gy * gy + gz * gz + 1.0)
            dipole = (
                spread[4 * chunks + h][None] * gx
                + spread[5 * chunks + h][None] * gy
                + spread[6 * chunks + h][None] * gz
            )
            acc = acc + inverse * (spread[3 * chunks + h][None] + dipole * (inverse * inverse))
        potential[at] = acc
        return 0

    lax.fori_loop(0, batches * points // 64, potential_of, 0)

    total[...] = jnp.zeros_like(total)
    for b in range(batches):
        field = potential[b * points // 8 : (b + 1) * points // 8].reshape(points, 128)
        hartree = jnp.sum(field, axis=1, keepdims=True)
        factor = features[:, b : b + 1] * (features[:, batches + b : batches + b + 1] + hartree)
        values = phi[b]
        scaled = (values.astype(F32) * factor).astype(BF16)
        for i in range(rel):
            term = lax.dot_general(
                scaled[:, i * 128 : (i + 1) * 128],
                values,
                (((0,), (0,)), ((), ())),
                preferred_element_type=F32,
            )
            for j in range(rel):
                q = needed[b * rel * rel + i * rel + j]
                total[q] += term[:, j * 128 : (j + 1) * 128]

    for q in range(total.shape[0]):
        w, k = place_of(q)
        for c in range(2):
            for y2 in range(2):
                first = c * 64 + y2 * 32
                out[(y2 * 2 + c) * 8 + w, k] = total[q, first : first + 32].astype(BF16)


def collect_kernel(ids, y2, received, out, total):
    total[...] = jnp.zeros_like(total)

    def add_one(n, _):
        near = ((n >> 4) ^ y2[0]) * 128 + (n & 15) * 8
        for k in range(8):
            block = jnp.maximum(ids[near + k], 0)
            total[(k // 2) * 8 + block] += received[n, k].astype(F32)
        return 0

    lax.fori_loop(0, received.shape[0], add_one, 0)
    for y4 in range(4):
        for z4 in range(4):
            for h in range(4):
                pair = jnp.concatenate(
                    [total[z4 * 8 + 2 * h + e, y4 * 8 : (y4 + 1) * 8] for e in range(2)], axis=0
                )
                out[y4 * 4 + z4, h * 16 : (h + 1) * 16] = pair.astype(BF16)


def on_device(
    basis_values,
    stored_density_blocks,
    device_request,
    batch_blocks,
    batch_atom,
    point_offset,
    point_weight,
    exchange_kernel,
    atom_xyz,
):
    batches, points, width = basis_values.shape
    own, tile = stored_density_blocks.shape[0], stored_density_blocks.shape[1]
    atoms = atom_xyz.shape[1]
    rel = width // tile
    padded = -(-atoms // 128) * 128
    c, y2, z4 = (lax.axis_index(a) for a in ("c", "y2", "z4"))
    half = tile // 2
    params = pltpu.CompilerParams(vmem_limit_bytes=40 * MIB)

    slab = lax.dynamic_slice_in_dim(stored_density_blocks, c * half, half, axis=1)
    pieces = [slab] + [lax.ppermute(slab, "z4", [(i, (i + s) % 4) for i in range(4)]) for s in (1, 2, 3)]
    wanted = device_request[0].reshape(4, 2, 4, 2).transpose(1, 2, 0, 3).reshape(1, 8, 8)
    wanted = jnp.broadcast_to(wanted, (2, 8, 8)).reshape(16, 8)
    ids = exchange(wanted, SERVE).reshape(-1)
    served = pl.pallas_call(
        serve_kernel,
        name="serve",
        out_shape=jax.ShapeDtypeStruct((16, 8, half, tile), BF16),
        in_specs=smem(2) + vmem(4),
        out_specs=vmem(1)[0],
        scratch_shapes=[pltpu.VMEM((4, own, half, tile), BF16)],
        compiler_params=params,
    )(ids, z4.reshape(1), *pieces)
    blocks = exchange(served, SERVE)
    near_ids = lax.ppermute(ids, "y2", [(0, 1), (1, 0)])
    both_ids = jnp.concatenate([ids, near_ids])

    needed = batch_blocks.reshape(-1)
    each = batches * VALUES
    density, share = pl.pallas_call(
        density_kernel,
        name="density",
        out_shape=(
            jax.ShapeDtypeStruct((batches, points), F32),
            jax.ShapeDtypeStruct((16, each), F32),
        ),
        in_specs=smem(2) + vmem(4),
        out_specs=tuple(vmem(2)),
        scratch_shapes=[pltpu.VMEM((2, width, width), BF16)],
        compiler_params=params,
    )(needed, batch_atom, basis_values, blocks, point_weight, point_offset)

    shares = exchange(share, GRP).reshape(1, 16 * each)
    shares = exchange(jnp.broadcast_to(shares, (32, 16 * each)), DEV)
    far = jnp.pad(atom_xyz, ((0, 0), (0, padded - atoms)))
    multipoles, outgoing = pl.pallas_call(
        term_kernel,
        name="terms",
        out_shape=(
            jax.ShapeDtypeStruct((VALUES, padded), F32),
            jax.ShapeDtypeStruct((32, 8, 32, tile), BF16),
        ),
        in_specs=smem(3) + vmem(7),
        out_specs=tuple(vmem(2)),
        scratch_shapes=[
            pltpu.VMEM((512, 128), F32),
            pltpu.VMEM((7 * padded // 128, 8, 128), F32),
            pltpu.VMEM((3, batches * points // 8, 8, 128), F32),
            pltpu.VMEM((batches * points // 8, 8, 128), F32),
            pltpu.VMEM((64, tile, tile), F32),
        ],
        compiler_params=params,
    )(
        needed,
        batch_atom,
        atom_xyz,
        shares,
        basis_values,
        density,
        point_weight,
        exchange_kernel,
        point_offset,
        far,
    )

    received = exchange(outgoing, COLLECT)
    partial = pl.pallas_call(
        collect_kernel,
        name="collect",
        out_shape=jax.ShapeDtypeStruct((16, own * 8, tile), BF16),
        in_specs=smem(2) + vmem(1),
        out_specs=vmem(1)[0],
        scratch_shapes=[pltpu.VMEM((4 * own, 32, tile), F32)],
        compiler_params=params,
    )(both_ids, y2.reshape(1), received)
    settled = exchange(partial, SETTLE).astype(F32).sum(axis=0).astype(BF16)
    rows = exchange(jnp.broadcast_to(settled[None], (16, own * 8, tile)), GRP)
    rows = rows.reshape(4, 2, 2, own, 8, tile).transpose(3, 2, 1, 0, 4, 5)
    return (rows.reshape(own, tile, tile), density, multipoles[:4, :atoms])


def solution(mesh):
    finer = Mesh(mesh.devices.reshape(4, 2, 2, 4, 2, 4), GRP_DEV)
    placed = (
        P(GRP_DEV, None, None),
        P(DEV, None, None),
        P(GRP_DEV, None, None),
        P(GRP_DEV, None),
        P(GRP_DEV),
        P(None, GRP_DEV, None),
        P(GRP_DEV, None),
        P(GRP_DEV, None),
        P(),
    )
    return jax.shard_map(
        on_device,
        mesh=finer,
        in_specs=placed,
        out_specs=(P(DEV, None, None), P(GRP_DEV, None), P()),
        check_vma=False,
    )
```

```python
import functools

import jax
import jax.numpy as jnp
from jax import lax
from jax.experimental import pallas as pl
from jax.experimental.pallas import tpu as pltpu
from jax.sharding import Mesh
from jax.sharding import PartitionSpec as P

GRP = ("y4", "y2", "c")
DEV = ("z4", "z2", "x")
GRP_DEV = GRP + DEV
SERVE = ("c", "z2", "x")
COLLECT = ("y2", "c", "z2", "x")
SETTLE = ("y4", "z4")

F32 = jnp.float32
BF16 = jnp.bfloat16
MIB = 1024 * 1024
VALUES = 8


def exchange(value, axes):
    return lax.all_to_all(value, axes, split_axis=0, concat_axis=0, tiled=True)


def vmem(count):
    return [pl.BlockSpec(memory_space=pltpu.VMEM)] * count


def smem(count):
    return [pl.BlockSpec(memory_space=pltpu.SMEM)] * count


def place_of(position):
    return (position >> 1) & 7, (position >> 4) * 2 + (position & 1)


def prepare_kernel(request, stored, message, slab, staged, sems):
    half = slab.shape[1]
    own = stored.at[:, pl.ds(pl.multiple_of(lax.axis_index("c") * half, half), half)]
    load = pltpu.make_async_copy(own, slab, sems.at[0])
    load.start()
    owners, slots = request.shape[1], request.shape[2]
    wide = jnp.pad(request[0], ((0, 128 - owners), (0, 128 - slots))).T
    flat = jnp.concatenate([wide[k : k + 1, :owners] for k in range(slots)], axis=1)
    flat = jnp.concatenate([flat, jnp.zeros((1, staged.shape[2] - owners * slots), jnp.int32)], axis=1)
    for n in range(staged.shape[0]):
        staged[n] = flat
    save = pltpu.make_async_copy(staged, message, sems.at[1])
    save.start()
    save.wait()
    load.wait()


def asked_at(asked, n, w, k):
    return jnp.maximum(asked[n, 0, (k % 2) * 32 + (k // 2) * 8 + w], 0)


def serve_kernel(message, own, one, two, three, out, kept, asked, held, ready, load_sems, sems):
    few = message.at[:, :, pl.ds(0, 128)]
    loads = [pltpu.make_async_copy(few, target, load_sems.at[n]) for n, target in enumerate((asked, kept))]
    for load in loads:
        load.start()
    z4 = lax.axis_index("z4")
    w = lax.axis_index("z2") * 4 + lax.axis_index("x")
    for shift, piece in enumerate((own, one, two, three)):
        held[(z4 - shift) & 3] = piece[...]
    for load in loads:
        load.wait()
    copies = []
    for n in range(ready.shape[0]):
        for k in range(8):
            ready[n, k] = held[k // 2, asked_at(asked, n, w, k)]
        copies.append(pltpu.make_async_copy(ready.at[n], out.at[n], sems.at[n]))
        copies[-1].start()
    for copy in copies:
        copy.wait()


def geometry_kernel(atom, places, offset, xyz, points_far, inverse_far, points_out, inverse_out, sems):
    batches, points = offset.shape[1], offset.shape[2]
    chunks = xyz.shape[1]
    filler = jnp.zeros((128 - 3 * batches, points), F32)
    features = jnp.concatenate([offset[0], offset[1], offset[2], filler], axis=0).T
    for b in range(batches):
        for k in range(3):
            spot = features[:, k * batches + b : k * batches + b + 1] + places[k, atom[b]]
            spot = jnp.broadcast_to(spot, (points, 128)).reshape(points // 8, 8, 128)
            points_out[k, b * points // 8 : (b + 1) * points // 8] = spot

    def inverse_of(step, _):
        at = pl.ds(step * 8, 8)
        px, py, pz = points_out[0, at], points_out[1, at], points_out[2, at]
        for h in range(chunks):
            gx = px - xyz[0, h : h + 1][None]
            gy = py - xyz[1, h : h + 1][None]
            gz = pz - xyz[2, h : h + 1][None]
            inverse_out[h, at] = lax.rsqrt(gx * gx + gy * gy + gz * gz + 1.0)
        return 0

    first = pltpu.make_async_copy(points_out, points_far, sems.at[0])
    first.start()
    lax.fori_loop(0, batches * points // 64, inverse_of, 0)
    second = pltpu.make_async_copy(inverse_out, inverse_far, sems.at[1])
    second.start()
    first.wait()
    second.wait()


def density_kernel(needed, atom, phi, blocks, weight, offset, rho_out, rho_again, share_out, wide):
    batches, points, width = phi.shape
    rel = width // 128
    half = blocks.shape[2]
    lane = lax.broadcasted_iota(jnp.int32, (points, 128), 1)
    columns = jnp.zeros((points, 128), F32)
    for b in range(batches):
        for p in range(rel * rel):
            w, k = place_of(needed[b * rel * rel + p])
            i, j = p // rel, p % rel
            for c in range(2):
                wide[b % 2, pl.ds(i * 128 + c * half, half), pl.ds(j * 128, 128)] = blocks[c * 8 + w, k]
        values = phi[b]
        product = jnp.dot(values, wide[b % 2], preferred_element_type=F32) * values.astype(F32)
        folded = product[:, :128]
        for j in range(1, rel):
            folded = folded + product[:, j * 128 : (j + 1) * 128]
        columns = jnp.where(lane == b, jnp.sum(folded, axis=1, keepdims=True), columns)
    rho = columns.T[:batches]
    rho_out[...] = rho
    rho_again[...] = rho
    weighted = rho * weight[...]
    moments = [weighted] + [weighted * offset[k] for k in range(3)]
    spot = lax.broadcasted_iota(jnp.int32, (batches, 128), 1)
    row = lax.broadcasted_iota(jnp.int32, (batches, 128), 0)
    tile = jnp.zeros((batches, 128), F32)
    for k, moment in enumerate(moments):
        tile = jnp.where(spot % VALUES == k, jnp.sum(moment, axis=1, keepdims=True), tile)
    for b in range(batches):
        mine = row == b
        tile = jnp.where((spot % VALUES == 4) & mine, (atom[b] & 127).astype(F32), tile)
        tile = jnp.where((spot % VALUES == 5) & mine, (atom[b] >> 7).astype(F32), tile)
    tile = jnp.where(spot // VALUES == row, tile, 0.0)
    flat = jnp.sum(tile, axis=0, keepdims=True)[:, : batches * VALUES]
    for n in range(share_out.shape[0]):
        share_out[n] = flat


def relay_kernel(near, out):
    row = jnp.concatenate([near[n] for n in range(near.shape[0])], axis=1)
    for n in range(out.shape[0]):
        out[n] = row


def term_kernel(
    needed,
    shares,
    rho,
    weight,
    exchange_part,
    xyz,
    points_from,
    inverse_from,
    phi_from,
    multipoles_out,
    out,
    points_at,
    inverse,
    phi,
    rows,
    spread,
    potential,
    total,
    ready,
    load_sems,
    sems,
):
    loads = [
        pltpu.make_async_copy(source, target, load_sems.at[n])
        for n, (source, target) in enumerate(((points_from, points_at), (inverse_from, inverse), (phi_from, phi)))
    ]
    for load in loads:
        load.start()
    batches, points, width = phi.shape
    rel = width // 128
    devices = rows.shape[0]
    sources = shares.shape[0]
    each = batches * VALUES
    chunks = xyz.shape[1]

    rows[...] = jnp.zeros_like(rows)
    near = shares[...].reshape(sources, shares.shape[2])
    for g in range(devices // sources):
        rows[g * sources : (g + 1) * sources, :each] = near[:, g * each : (g + 1) * each]
    table = rows[...]
    turned = table.T
    low_at = lax.broadcasted_iota(jnp.int32, (devices, 128), 1).astype(F32)
    high_at = lax.broadcasted_iota(jnp.int32, (chunks, devices), 0).astype(F32)
    summed = jnp.zeros((12 * chunks, 128), F32)
    for b in range(batches):
        low = jnp.where(table[:, b * VALUES + 4 : b * VALUES + 5] == low_at, 1.0, 0.0).astype(BF16)
        high = jnp.where(turned[b * VALUES + 5 : b * VALUES + 6] == high_at, 1.0, 0.0)
        rest = turned[b * VALUES : (b + 1) * VALUES]
        stacked = []
        for _ in range(3):
            part = rest.astype(BF16).astype(F32)
            rest = rest - part
            stacked += [high * part[k : k + 1] for k in range(4)]
        stacked = jnp.concatenate(stacked, axis=0).astype(BF16)
        summed = summed + jnp.dot(stacked, low, preferred_element_type=F32)
    multipoles = [
        summed[k * chunks : (k + 1) * chunks]
        + (summed[(4 + k) * chunks : (5 + k) * chunks] + summed[(8 + k) * chunks : (9 + k) * chunks])
        for k in range(4)
    ]
    for k in range(4):
        multipoles_out[k * chunks : (k + 1) * chunks] = multipoles[k]
    shift = multipoles[1] * xyz[0] + multipoles[2] * xyz[1] + multipoles[3] * xyz[2]
    for k, value in enumerate(multipoles + [shift]):
        for h in range(chunks):
            spread[k * chunks + h] = jnp.broadcast_to(value[h : h + 1], (8, 128))

    loads[0].wait()
    loads[1].wait()

    def potential_of(step, _):
        at = pl.ds(step * 8, 8)
        px, py, pz = points_at[0, at], points_at[1, at], points_at[2, at]
        acc = jnp.zeros((8, 8, 128), F32)
        for h in range(chunks):
            dipole = (
                spread[chunks + h][None] * px
                + spread[2 * chunks + h][None] * py
                + spread[3 * chunks + h][None] * pz
                - spread[4 * chunks + h][None]
            )
            s = inverse[h, at]
            acc = acc + s * (spread[h][None] + dipole * (s * s))
        potential[at] = acc
        return 0

    lax.fori_loop(0, batches * points // 64, potential_of, 0)

    filler = jnp.zeros((128 - 2 * batches, points), F32)
    features = jnp.concatenate([weight[...], exchange_part[...] * rho[...], filler], axis=0).T
    total[...] = jnp.zeros_like(total)
    loads[2].wait()
    for b in range(batches):
        field = potential[b * points // 8 : (b + 1) * points // 8].reshape(points, 128)
        hartree = jnp.sum(field, axis=1, keepdims=True)
        factor = features[:, b : b + 1] * (features[:, batches + b : batches + b + 1] + hartree)
        values = phi[b]
        scaled = (values.astype(F32) * factor).astype(BF16)
        for i in range(rel):
            term = lax.dot_general(
                scaled[:, i * 128 : (i + 1) * 128],
                values,
                (((0,), (0,)), ((), ())),
                preferred_element_type=F32,
            )
            for j in range(rel):
                q = needed[b * rel * rel + i * rel + j]
                total[q] += term[:, j * 128 : (j + 1) * 128]

    copies = []
    for w in range(8):
        for k in range(8):
            q = (k // 2) * 16 + w * 2 + k % 2
            for c in range(2):
                for y2 in range(2):
                    first = c * 64 + y2 * 32
                    ready[(y2 * 2 + c) * 8 + w, k] = total[q, first : first + 32].astype(BF16)
        for d in range(w, 32, 8):
            copies.append(pltpu.make_async_copy(ready.at[d], out.at[d], sems.at[d]))
            copies[-1].start()
    for copy in copies:
        copy.wait()


def collect_kernel(asked, asked_near, received, out, total):
    total[...] = jnp.zeros_like(total)
    w = lax.axis_index("z2") * 4 + lax.axis_index("x")
    y2 = lax.axis_index("y2")

    def add_one(n, _):
        mine = (n >> 4) == y2
        for k in range(8):
            block = jnp.where(mine, asked_at(asked, n & 15, w, k), asked_at(asked_near, n & 15, w, k))
            total[(k // 2) * 8 + block] += received[n, k].astype(F32)
        return 0

    lax.fori_loop(0, received.shape[0], add_one, 0)
    for y4 in range(4):
        for z4 in range(4):
            for h in range(4):
                pair = jnp.concatenate(
                    [total[z4 * 8 + 2 * h + e, y4 * 8 : (y4 + 1) * 8] for e in range(2)], axis=0
                )
                out[y4 * 4 + z4, h * 16 : (h + 1) * 16] = pair.astype(BF16)


def on_device(
    basis_values,
    stored_density_blocks,
    device_request,
    batch_blocks,
    batch_atom,
    point_offset,
    point_weight,
    exchange_kernel,
    atom_xyz,
):
    batches, points, width = basis_values.shape
    own, tile = stored_density_blocks.shape[0], stored_density_blocks.shape[1]
    atoms = atom_xyz.shape[1]
    padded = -(-atoms // 128) * 128
    half = tile // 2
    chunks = padded // 128
    each = batches * VALUES
    groups = batches * points // 8
    params = pltpu.CompilerParams(vmem_limit_bytes=32 * MIB)
    hbm = pl.BlockSpec(memory_space=pltpu.HBM)
    far_away = pl.BlockSpec(memory_space=pl.ANY)

    far = jnp.pad(atom_xyz, ((0, 0), (0, padded - atoms))).reshape(3, chunks, 128)
    points_at, inverse = pl.pallas_call(
        geometry_kernel,
        name="geometry",
        out_shape=(
            pltpu.HBM((3, groups, 8, 128), F32),
            pltpu.HBM((chunks, groups, 8, 128), F32),
        ),
        in_specs=smem(2) + vmem(2),
        out_specs=(hbm, hbm),
        scratch_shapes=[
            pltpu.VMEM((3, groups, 8, 128), F32),
            pltpu.VMEM((chunks, groups, 8, 128), F32),
            pltpu.SemaphoreType.DMA((2,)),
        ],
        compiler_params=params,
        cost_estimate=pl.CostEstimate(flops=2 * 10**7, bytes_accessed=6 * MIB, transcendentals=10**6),
    )(batch_atom, atom_xyz, point_offset, far)

    message, slab = pl.pallas_call(
        prepare_kernel,
        name="prepare",
        out_shape=(pltpu.HBM((16, 1, 2048), jnp.int32), jax.ShapeDtypeStruct((own, half, tile), BF16)),
        in_specs=vmem(1) + [hbm],
        out_specs=(hbm, vmem(1)[0]),
        scratch_shapes=[pltpu.VMEM((16, 1, 2048), jnp.int32), pltpu.SemaphoreType.DMA((2,))],
        compiler_params=params,
    )(device_request, pltpu.with_memory_space_constraint(stored_density_blocks, pltpu.HBM))
    message = exchange(message, SERVE)
    pieces = [slab] + [lax.ppermute(slab, "z4", [(i, (i + s) % 4) for i in range(4)]) for s in (1, 2, 3)]
    served, asked = pl.pallas_call(
        serve_kernel,
        name="serve",
        out_shape=(pltpu.HBM((16, 8, half, tile), BF16), jax.ShapeDtypeStruct((16, 1, 128), jnp.int32)),
        in_specs=[far_away] + vmem(4),
        out_specs=(hbm, vmem(1)[0]),
        scratch_shapes=[
            pltpu.SMEM((16, 1, 128), jnp.int32),
            pltpu.VMEM((4, own, half, tile), BF16),
            pltpu.VMEM((16, 8, half, tile), BF16),
            pltpu.SemaphoreType.DMA((2,)),
            pltpu.SemaphoreType.DMA((16,)),
        ],
        compiler_params=params,
    )(message, *pieces)
    blocks = exchange(served, SERVE)
    asked_near = lax.ppermute(asked, "y2", [(0, 1), (1, 0)])

    needed = batch_blocks.reshape(-1)
    density, density_again, share = pl.pallas_call(
        density_kernel,
        name="density",
        out_shape=(
            jax.ShapeDtypeStruct((batches, points), F32),
            jax.ShapeDtypeStruct((batches, points), F32),
            jax.ShapeDtypeStruct((16, 1, each), F32),
        ),
        in_specs=smem(2) + vmem(4),
        out_specs=tuple(vmem(3)),
        scratch_shapes=[pltpu.VMEM((2, width, width), BF16)],
        compiler_params=params,
    )(needed, batch_atom, basis_values, blocks, point_weight, point_offset)

    shares = pl.pallas_call(
        relay_kernel,
        name="relay",
        out_shape=jax.ShapeDtypeStruct((32, 1, 16 * each), F32),
        in_specs=vmem(1),
        out_specs=vmem(1)[0],
        compiler_params=params,
    )(exchange(share, GRP))
    multipoles, outgoing = pl.pallas_call(
        term_kernel,
        name="terms",
        out_shape=(
            jax.ShapeDtypeStruct((4 * chunks, 128), F32),
            pltpu.HBM((32, 8, 32, tile), BF16),
        ),
        in_specs=smem(1) + vmem(5) + [hbm, hbm, far_away],
        out_specs=(vmem(1)[0], hbm),
        scratch_shapes=[
            pltpu.VMEM(points_at.shape, F32),
            pltpu.VMEM(inverse.shape, F32),
            pltpu.VMEM(basis_values.shape, BF16),
            pltpu.VMEM((512, 128), F32),
            pltpu.VMEM((5 * chunks, 8, 128), F32),
            pltpu.VMEM((groups, 8, 128), F32),
            pltpu.VMEM((64, tile, tile), F32),
            pltpu.VMEM((32, 8, 32, tile), BF16),
            pltpu.SemaphoreType.DMA((3,)),
            pltpu.SemaphoreType.DMA((32,)),
        ],
        compiler_params=params,
    )(
        needed,
        exchange(shares, DEV),
        density_again,
        point_weight,
        exchange_kernel,
        far,
        pltpu.with_memory_space_constraint(points_at, pltpu.HBM),
        pltpu.with_memory_space_constraint(inverse, pltpu.HBM),
        basis_values,
    )

    received = exchange(outgoing, COLLECT)
    partial = pl.pallas_call(
        collect_kernel,
        name="collect",
        out_shape=jax.ShapeDtypeStruct((16, own * 8, tile), BF16),
        in_specs=smem(2) + vmem(1),
        out_specs=vmem(1)[0],
        scratch_shapes=[pltpu.VMEM((4 * own, 32, tile), F32)],
        compiler_params=params,
    )(asked, asked_near, received)
    settled = exchange(partial, SETTLE).astype(F32).sum(axis=0).astype(BF16)
    rows = exchange(jnp.broadcast_to(settled[None], (16, own * 8, tile)), GRP)
    rows = rows.reshape(4, 2, 2, own, 8, tile).transpose(3, 2, 1, 0, 4, 5)
    return (rows.reshape(own, tile, tile), density, multipoles.reshape(4, padded)[:, :atoms])


def solution(mesh):
    finer = Mesh(mesh.devices.reshape(4, 2, 2, 4, 2, 4), GRP_DEV)
    placed = (
        P(GRP_DEV, None, None),
        P(DEV, None, None),
        P(GRP_DEV, None, None),
        P(GRP_DEV, None),
        P(GRP_DEV),
        P(None, GRP_DEV, None),
        P(GRP_DEV, None),
        P(GRP_DEV, None),
        P(),
    )
    return jax.shard_map(
        on_device,
        mesh=finer,
        in_specs=placed,
        out_specs=(P(DEV, None, None), P(GRP_DEV, None), P()),
        check_vma=False,
    )
```

```python
import functools

import jax
import jax.numpy as jnp
from jax import lax
from jax.experimental import pallas as pl
from jax.experimental.pallas import tpu as pltpu
from jax.sharding import Mesh
from jax.sharding import PartitionSpec as P

GRP = ("y4", "y2", "c")
DEV = ("z4", "z2", "x")
GRP_DEV = GRP + DEV
COLLECT = ("y2", "c", "z2", "x")
SETTLE = ("y4", "z4")

F32 = jnp.float32
BF16 = jnp.bfloat16
MIB = 1024 * 1024
VALUES = 8


def exchange(value, axes):
    return lax.all_to_all(value, axes, split_axis=0, concat_axis=0, tiled=True)


def vmem(count):
    return [pl.BlockSpec(memory_space=pltpu.VMEM)] * count


def smem(count):
    return [pl.BlockSpec(memory_space=pltpu.SMEM)] * count


def place_of(position):
    return (position >> 1) & 7, (position >> 4) * 2 + (position & 1)


def prepare_kernel(request, stored, message, slab, staged, sems):
    part = slab.shape[1]
    at = (lax.axis_index("c") * 2 + lax.axis_index("y2")) * part
    own = stored.at[:, pl.ds(pl.multiple_of(at, part), part)]
    load = pltpu.make_async_copy(own, slab, sems.at[0])
    load.start()
    owners, slots = request.shape[1], request.shape[2]
    wide = jnp.pad(request[0], ((0, 128 - owners), (0, 128 - slots))).T
    flat = jnp.concatenate([wide[k : k + 1, :owners] for k in range(slots)], axis=1)
    flat = jnp.concatenate([flat, jnp.zeros((1, staged.shape[2] - owners * slots), jnp.int32)], axis=1)
    for n in range(staged.shape[0]):
        staged[n] = flat
    save = pltpu.make_async_copy(staged, message, sems.at[1])
    save.start()
    save.wait()
    load.wait()


def asked_at(asked, n, w, k):
    return jnp.maximum(asked[n, 0, (k % 2) * 32 + (k // 2) * 8 + w], 0)


def serve_kernel(message, own, one, two, three, out, kept, asked, held, ready, load_sems, sems):
    few = message.at[:, :, pl.ds(0, 128)]
    loads = [pltpu.make_async_copy(few, target, load_sems.at[n]) for n, target in enumerate((asked, kept))]
    for load in loads:
        load.start()
    z4 = lax.axis_index("z4")
    w = lax.axis_index("z2") * 4 + lax.axis_index("x")
    for shift, piece in enumerate((own, one, two, three)):
        held[(z4 - shift) & 3] = piece[...]
    for load in loads:
        load.wait()
    copies = []
    for n in range(ready.shape[0]):
        for k in range(8):
            ready[n, k] = held[k // 2, asked_at(asked, n, w, k)]
        copies.append(pltpu.make_async_copy(ready.at[n], out.at[n], sems.at[n]))
        copies[-1].start()
    for copy in copies:
        copy.wait()


def geometry_kernel(atom, places, offset, xyz, points_out, inverse_far, inverse, sems):
    batches, points = offset.shape[1], offset.shape[2]
    chunks = xyz.shape[1]
    rows = points // 8
    filler = jnp.zeros((128 - 3 * batches, points), F32)
    features = jnp.concatenate([offset[0], offset[1], offset[2], filler], axis=0).T
    copies = []
    for b in range(batches):
        for k in range(3):
            spot = features[:, k * batches + b : k * batches + b + 1] + places[k, atom[b]]
            points_out[k, b * rows : (b + 1) * rows] = jnp.broadcast_to(spot, (points, 128)).reshape(rows, 8, 128)

        def inverse_of(step, _, b=b):
            at = pl.ds(step * 8, 8)
            px, py, pz = (points_out[k, pl.ds(b * rows + step * 8, 8)] for k in range(3))
            for h in range(chunks):
                gx = px - xyz[0, h : h + 1][None]
                gy = py - xyz[1, h : h + 1][None]
                gz = pz - xyz[2, h : h + 1][None]
                inverse[b, h, at] = lax.rsqrt(gx * gx + gy * gy + gz * gz + 1.0)
            return 0

        lax.fori_loop(0, rows // 8, inverse_of, 0)
        copies.append(pltpu.make_async_copy(inverse.at[b], inverse_far.at[b], sems.at[b]))
        copies[-1].start()
    for copy in copies:
        copy.wait()


def density_kernel(needed, atom, phi, blocks, weight, offset, rho_out, rho_again, share_out, wide):
    batches, points, width = phi.shape
    rel = width // 128
    part = blocks.shape[2]
    lane = lax.broadcasted_iota(jnp.int32, (points, 128), 1)
    columns = jnp.zeros((points, 128), F32)
    for b in range(batches):
        for p in range(rel * rel):
            w, k = place_of(needed[b * rel * rel + p])
            i, j = p // rel, p % rel
            for c in range(2):
                for y2 in range(2):
                    at = i * 128 + (c * 2 + y2) * part
                    wide[b % 2, pl.ds(at, part), pl.ds(j * 128, 128)] = blocks[(y2 * 2 + c) * 8 + w, k]
        values = phi[b]
        product = jnp.dot(values, wide[b % 2], preferred_element_type=F32) * values.astype(F32)
        folded = product[:, :128]
        for j in range(1, rel):
            folded = folded + product[:, j * 128 : (j + 1) * 128]
        columns = jnp.where(lane == b, jnp.sum(folded, axis=1, keepdims=True), columns)
    rho = columns.T[:batches]
    rho_out[...] = rho
    rho_again[...] = rho
    weighted = rho * weight[...]
    moments = [weighted] + [weighted * offset[k] for k in range(3)]
    spot = lax.broadcasted_iota(jnp.int32, (batches, 128), 1)
    row = lax.broadcasted_iota(jnp.int32, (batches, 128), 0)
    tile = jnp.zeros((batches, 128), F32)
    for k, moment in enumerate(moments):
        tile = jnp.where(spot % VALUES == k, jnp.sum(moment, axis=1, keepdims=True), tile)
    for b in range(batches):
        mine = row == b
        tile = jnp.where((spot % VALUES == 4) & mine, (atom[b] & 127).astype(F32), tile)
        tile = jnp.where((spot % VALUES == 5) & mine, (atom[b] >> 7).astype(F32), tile)
    tile = jnp.where(spot // VALUES == row, tile, 0.0)
    flat = jnp.sum(tile, axis=0, keepdims=True)[:, : batches * VALUES]
    for n in range(share_out.shape[0]):
        share_out[n] = flat


def relay_kernel(near, out):
    row = jnp.concatenate([near[n] for n in range(near.shape[0])], axis=1)
    for n in range(out.shape[0]):
        out[n] = row


def term_kernel(
    needed,
    shares,
    rho,
    weight,
    exchange_part,
    xyz,
    points_at,
    phi,
    inverse_far,
    multipoles_out,
    out,
    inverse,
    rows,
    spread,
    potential,
    total,
    load_sems,
):
    loads = [pltpu.make_async_copy(inverse_far.at[b], inverse.at[b], load_sems.at[b]) for b in range(phi.shape[0])]
    for load in loads:
        load.start()
    batches, points, width = phi.shape
    rel = width // 128
    devices = rows.shape[0]
    sources = shares.shape[0]
    each = batches * VALUES
    chunks = xyz.shape[1]

    rows[...] = jnp.zeros_like(rows)
    near = shares[...].reshape(sources, shares.shape[2])
    for g in range(devices // sources):
        rows[g * sources : (g + 1) * sources, :each] = near[:, g * each : (g + 1) * each]
    table = rows[...]
    turned = table.T
    low_at = lax.broadcasted_iota(jnp.int32, (devices, 128), 1).astype(F32)
    high_at = lax.broadcasted_iota(jnp.int32, (chunks, devices), 0).astype(F32)
    summed = jnp.zeros((12 * chunks, 128), F32)
    for b in range(batches):
        low = jnp.where(table[:, b * VALUES + 4 : b * VALUES + 5] == low_at, 1.0, 0.0).astype(BF16)
        high = jnp.where(turned[b * VALUES + 5 : b * VALUES + 6] == high_at, 1.0, 0.0)
        rest = turned[b * VALUES : (b + 1) * VALUES]
        stacked = []
        for _ in range(3):
            part = rest.astype(BF16).astype(F32)
            rest = rest - part
            stacked += [high * part[k : k + 1] for k in range(4)]
        stacked = jnp.concatenate(stacked, axis=0).astype(BF16)
        summed = summed + jnp.dot(stacked, low, preferred_element_type=F32)
    multipoles = [
        summed[k * chunks : (k + 1) * chunks]
        + (summed[(4 + k) * chunks : (5 + k) * chunks] + summed[(8 + k) * chunks : (9 + k) * chunks])
        for k in range(4)
    ]
    for k in range(4):
        multipoles_out[k * chunks : (k + 1) * chunks] = multipoles[k]
    shift = multipoles[1] * xyz[0] + multipoles[2] * xyz[1] + multipoles[3] * xyz[2]
    for k, value in enumerate(multipoles + [shift]):
        for h in range(chunks):
            spread[k * chunks + h] = jnp.broadcast_to(value[h : h + 1], (8, 128))

    filler = jnp.zeros((128 - 2 * batches, points), F32)
    features = jnp.concatenate([weight[...], exchange_part[...] * rho[...], filler], axis=0).T
    total[...] = jnp.zeros_like(total)
    rows_each = points // 8
    for b in range(batches):
        loads[b].wait()

        def potential_of(step, _, b=b):
            at = pl.ds(step * 8, 8)
            px, py, pz = (points_at[k, pl.ds(b * rows_each + step * 8, 8)] for k in range(3))
            acc = jnp.zeros((8, 8, 128), F32)
            for h in range(chunks):
                dipole = (
                    spread[chunks + h][None] * px
                    + spread[2 * chunks + h][None] * py
                    + spread[3 * chunks + h][None] * pz
                    - spread[4 * chunks + h][None]
                )
                s = inverse[b, h, at]
                acc = acc + s * (spread[h][None] + dipole * (s * s))
            potential[at] = acc
            return 0

        lax.fori_loop(0, rows_each // 8, potential_of, 0)
        hartree = jnp.sum(potential[...].reshape(points, 128), axis=1, keepdims=True)
        factor = features[:, b : b + 1] * (features[:, batches + b : batches + b + 1] + hartree)
        values = phi[b]
        scaled = (values.astype(F32) * factor).astype(BF16)
        for i in range(rel):
            term = lax.dot_general(
                scaled[:, i * 128 : (i + 1) * 128],
                values,
                (((0,), (0,)), ((), ())),
                preferred_element_type=F32,
            )
            for j in range(rel):
                q = needed[b * rel * rel + i * rel + j]
                total[q] += term[:, j * 128 : (j + 1) * 128]

    for w in range(8):
        for k in range(8):
            q = (k // 2) * 16 + w * 2 + k % 2
            for c in range(2):
                for y2 in range(2):
                    first = c * 64 + y2 * 32
                    out[(y2 * 2 + c) * 8 + w, k] = total[q, first : first + 32].astype(BF16)


def collect_kernel(asked, received, out, total):
    total[...] = jnp.zeros_like(total)
    w = lax.axis_index("z2") * 4 + lax.axis_index("x")

    def add_one(n, _):
        for k in range(8):
            total[(k // 2) * 8 + asked_at(asked, n, w, k)] += received[n, k].astype(F32)
        return 0

    lax.fori_loop(0, received.shape[0], add_one, 0)
    for y4 in range(4):
        for z4 in range(4):
            for h in range(4):
                pair = jnp.concatenate(
                    [total[z4 * 8 + 2 * h + e, y4 * 8 : (y4 + 1) * 8] for e in range(2)], axis=0
                )
                out[y4 * 4 + z4, h * 16 : (h + 1) * 16] = pair.astype(BF16)


def on_device(
    basis_values,
    stored_density_blocks,
    device_request,
    batch_blocks,
    batch_atom,
    point_offset,
    point_weight,
    exchange_kernel,
    atom_xyz,
):
    batches, points, width = basis_values.shape
    own, tile = stored_density_blocks.shape[0], stored_density_blocks.shape[1]
    atoms = atom_xyz.shape[1]
    padded = -(-atoms // 128) * 128
    part = tile // 4
    chunks = padded // 128
    each = batches * VALUES
    groups = batches * points // 8
    params = pltpu.CompilerParams(vmem_limit_bytes=32 * MIB)
    hbm = pl.BlockSpec(memory_space=pltpu.HBM)
    far_away = pl.BlockSpec(memory_space=pl.ANY)

    far = jnp.pad(atom_xyz, ((0, 0), (0, padded - atoms))).reshape(3, chunks, 128)
    points_at, inverse = pl.pallas_call(
        geometry_kernel,
        name="geometry",
        out_shape=(
            pltpu.VMEM((3, groups, 8, 128), F32),
            pltpu.HBM((batches, chunks, points // 8, 8, 128), F32),
        ),
        in_specs=smem(2) + vmem(2),
        out_specs=(vmem(1)[0], hbm),
        scratch_shapes=[
            pltpu.VMEM((batches, chunks, points // 8, 8, 128), F32),
            pltpu.SemaphoreType.DMA((batches,)),
        ],
        compiler_params=params,
        cost_estimate=pl.CostEstimate(flops=2 * 10**7, bytes_accessed=6 * MIB, transcendentals=10**6),
    )(batch_atom, atom_xyz, point_offset, far)

    message, slab = pl.pallas_call(
        prepare_kernel,
        name="prepare",
        out_shape=(pltpu.HBM((32, 1, 1024), jnp.int32), jax.ShapeDtypeStruct((own, part, tile), BF16)),
        in_specs=vmem(1) + [hbm],
        out_specs=(hbm, vmem(1)[0]),
        scratch_shapes=[pltpu.VMEM((32, 1, 1024), jnp.int32), pltpu.SemaphoreType.DMA((2,))],
        compiler_params=params,
    )(device_request, pltpu.with_memory_space_constraint(stored_density_blocks, pltpu.HBM))
    message = exchange(message, COLLECT)
    pieces = [slab] + [lax.ppermute(slab, "z4", [(i, (i + s) % 4) for i in range(4)]) for s in (1, 2, 3)]
    served, asked = pl.pallas_call(
        serve_kernel,
        name="serve",
        out_shape=(pltpu.HBM((32, 8, part, tile), BF16), jax.ShapeDtypeStruct((32, 1, 128), jnp.int32)),
        in_specs=[far_away] + vmem(4),
        out_specs=(hbm, vmem(1)[0]),
        scratch_shapes=[
            pltpu.SMEM((32, 1, 128), jnp.int32),
            pltpu.VMEM((4, own, part, tile), BF16),
            pltpu.VMEM((32, 8, part, tile), BF16),
            pltpu.SemaphoreType.DMA((2,)),
            pltpu.SemaphoreType.DMA((32,)),
        ],
        compiler_params=params,
    )(message, *pieces)
    blocks = exchange(served, COLLECT)

    needed = batch_blocks.reshape(-1)
    density, density_again, share = pl.pallas_call(
        density_kernel,
        name="density",
        out_shape=(
            jax.ShapeDtypeStruct((batches, points), F32),
            jax.ShapeDtypeStruct((batches, points), F32),
            jax.ShapeDtypeStruct((32, 1, each), F32),
        ),
        in_specs=smem(2) + vmem(4),
        out_specs=tuple(vmem(3)),
        scratch_shapes=[pltpu.VMEM((2, width, width), BF16)],
        compiler_params=params,
    )(needed, batch_atom, basis_values, blocks, point_weight, point_offset)

    shares = pl.pallas_call(
        relay_kernel,
        name="relay",
        out_shape=jax.ShapeDtypeStruct((16, 1, 32 * each), F32),
        in_specs=vmem(1),
        out_specs=vmem(1)[0],
        compiler_params=params,
    )(exchange(share, COLLECT))
    multipoles, outgoing = pl.pallas_call(
        term_kernel,
        name="terms",
        out_shape=(
            jax.ShapeDtypeStruct((4 * chunks, 128), F32),
            jax.ShapeDtypeStruct((32, 8, 32, tile), BF16),
        ),
        in_specs=smem(1) + vmem(7) + [hbm],
        out_specs=tuple(vmem(2)),
        scratch_shapes=[
            pltpu.VMEM(inverse.shape, F32),
            pltpu.VMEM((512, 128), F32),
            pltpu.VMEM((5 * chunks, 8, 128), F32),
            pltpu.VMEM((points // 8, 8, 128), F32),
            pltpu.VMEM((64, tile, tile), F32),
            pltpu.SemaphoreType.DMA((batches,)),
        ],
        compiler_params=params,
    )(
        needed,
        exchange(shares, SETTLE),
        density_again,
        point_weight,
        exchange_kernel,
        far,
        pltpu.with_memory_space_constraint(points_at, pltpu.VMEM),
        basis_values,
        pltpu.with_memory_space_constraint(inverse, pltpu.HBM),
    )

    received = exchange(outgoing, COLLECT)
    partial = pl.pallas_call(
        collect_kernel,
        name="collect",
        out_shape=jax.ShapeDtypeStruct((16, own * 8, tile), BF16),
        in_specs=smem(1) + vmem(1),
        out_specs=vmem(1)[0],
        scratch_shapes=[pltpu.VMEM((4 * own, 32, tile), F32)],
        compiler_params=params,
    )(asked, received)
    settled = exchange(partial, SETTLE).astype(F32).sum(axis=0).astype(BF16)
    rows = exchange(jnp.broadcast_to(settled[None], (16, own * 8, tile)), GRP)
    rows = rows.reshape(4, 2, 2, own, 8, tile).transpose(3, 2, 1, 0, 4, 5)
    return (rows.reshape(own, tile, tile), density, multipoles.reshape(4, padded)[:, :atoms])


def solution(mesh):
    finer = Mesh(mesh.devices.reshape(4, 2, 2, 4, 2, 4), GRP_DEV)
    placed = (
        P(GRP_DEV, None, None),
        P(DEV, None, None),
        P(GRP_DEV, None, None),
        P(GRP_DEV, None),
        P(GRP_DEV),
        P(None, GRP_DEV, None),
        P(GRP_DEV, None),
        P(GRP_DEV, None),
        P(),
    )
    return jax.shard_map(
        on_device,
        mesh=finer,
        in_specs=placed,
        out_specs=(P(DEV, None, None), P(GRP_DEV, None), P()),
        check_vma=False,
    )
```

```python
import functools

import jax
import jax.numpy as jnp
from jax import lax
from jax.experimental import pallas as pl
from jax.experimental.pallas import tpu as pltpu
from jax.sharding import Mesh
from jax.sharding import PartitionSpec as P

GRP = ("y4", "y2", "c")
DEV = ("z4", "z2", "x")
GRP_DEV = GRP + DEV
COLLECT = ("y2", "c", "z2", "x")
SETTLE = ("y4", "z4")

F32 = jnp.float32
BF16 = jnp.bfloat16
MIB = 1024 * 1024
VALUES = 8


def exchange(value, axes):
    return lax.all_to_all(value, axes, split_axis=0, concat_axis=0, tiled=True)


def vmem(count):
    return [pl.BlockSpec(memory_space=pltpu.VMEM)] * count


def smem(count):
    return [pl.BlockSpec(memory_space=pltpu.SMEM)] * count


def place_of(position):
    return (position >> 1) & 7, (position >> 4) * 2 + (position & 1)


def prepare_kernel(request_far, stored, message, slab, request, staged, sems):
    ask = pltpu.make_async_copy(request_far, request, sems.at[2])
    ask.start()
    part = slab.shape[1]
    at = (lax.axis_index("c") * 2 + lax.axis_index("y2")) * part
    own = stored.at[:, pl.ds(pl.multiple_of(at, part), part)]
    load = pltpu.make_async_copy(own, slab, sems.at[0])
    load.start()
    slots, owners = request.shape[1], request.shape[2]
    ask.wait()
    flat = jnp.concatenate([request[0, k : k + 1] for k in range(slots)], axis=1)
    flat = jnp.concatenate([flat, jnp.zeros((1, staged.shape[2] - owners * slots), jnp.int32)], axis=1)
    for n in range(staged.shape[0]):
        staged[n] = flat
    save = pltpu.make_async_copy(staged, message, sems.at[1])
    save.start()
    save.wait()
    load.wait()


def asked_at(asked, n, w, k):
    return jnp.maximum(asked[n, 0, (k % 2) * 32 + (k // 2) * 8 + w], 0)


def serve_kernel(message, own, one, two, three, out, kept, asked, held, load_sems):
    few = message.at[:, :, pl.ds(0, 128)]
    loads = [pltpu.make_async_copy(few, target, load_sems.at[n]) for n, target in enumerate((asked, kept))]
    for load in loads:
        load.start()
    z4 = lax.axis_index("z4")
    w = lax.axis_index("z2") * 4 + lax.axis_index("x")
    for shift, piece in enumerate((own, one, two, three)):
        held[(z4 - shift) & 3] = piece[...]
    for load in loads:
        load.wait()
    for n in range(out.shape[0]):
        for k in range(8):
            out[n, k] = held[k // 2, asked_at(asked, n, w, k)]


def geometry_kernel(atom, places, offset, xyz, points_out, inverse_far, inverse, sems):
    batches, points = offset.shape[1], offset.shape[2]
    chunks = xyz.shape[1]
    rows = points // 8
    filler = jnp.zeros((128 - 3 * batches, points), F32)
    features = jnp.concatenate([offset[0], offset[1], offset[2], filler], axis=0).T
    copies = []
    for b in range(batches):
        for k in range(3):
            spot = features[:, k * batches + b : k * batches + b + 1] + places[k, atom[b]]
            points_out[k, b * rows : (b + 1) * rows] = jnp.broadcast_to(spot, (points, 128)).reshape(rows, 8, 128)

        def inverse_of(step, _, b=b):
            at = pl.ds(step * 8, 8)
            px, py, pz = (points_out[k, pl.ds(b * rows + step * 8, 8)] for k in range(3))
            for h in range(chunks):
                gx = px - xyz[0, h : h + 1][None]
                gy = py - xyz[1, h : h + 1][None]
                gz = pz - xyz[2, h : h + 1][None]
                inverse[b, h, at] = lax.rsqrt(gx * gx + gy * gy + gz * gz + 1.0)
            return 0

        lax.fori_loop(0, rows // 8, inverse_of, 0)
        copies.append(pltpu.make_async_copy(inverse.at[b], inverse_far.at[b], sems.at[b]))
        copies[-1].start()
    for copy in copies:
        copy.wait()


def density_kernel(needed, atom, phi, blocks, weight, offset, rho_out, rho_again, share_out, wide):
    batches, points, width = phi.shape
    rel = width // 128
    part = blocks.shape[2]
    lane = lax.broadcasted_iota(jnp.int32, (points, 128), 1)
    columns = jnp.zeros((points, 128), F32)
    for b in range(batches):
        for p in range(rel * rel):
            w, k = place_of(needed[b, p])
            i, j = p // rel, p % rel
            for c in range(2):
                for y2 in range(2):
                    at = i * 128 + (c * 2 + y2) * part
                    wide[b % 2, pl.ds(at, part), pl.ds(j * 128, 128)] = blocks[(y2 * 2 + c) * 8 + w, k]
        values = phi[b]
        product = jnp.dot(values, wide[b % 2], preferred_element_type=F32) * values.astype(F32)
        folded = product[:, :128]
        for j in range(1, rel):
            folded = folded + product[:, j * 128 : (j + 1) * 128]
        columns = jnp.where(lane == b, jnp.sum(folded, axis=1, keepdims=True), columns)
    rho = columns.T[:batches]
    rho_out[...] = rho
    rho_again[...] = rho
    weighted = rho * weight[...]
    moments = [weighted] + [weighted * offset[k] for k in range(3)]
    spot = lax.broadcasted_iota(jnp.int32, (batches, 128), 1)
    row = lax.broadcasted_iota(jnp.int32, (batches, 128), 0)
    tile = jnp.zeros((batches, 128), F32)
    for k, moment in enumerate(moments):
        tile = jnp.where(spot % VALUES == k, jnp.sum(moment, axis=1, keepdims=True), tile)
    for b in range(batches):
        mine = row == b
        tile = jnp.where((spot % VALUES == 4) & mine, (atom[b] & 127).astype(F32), tile)
        tile = jnp.where((spot % VALUES == 5) & mine, (atom[b] >> 7).astype(F32), tile)
    tile = jnp.where(spot // VALUES == row, tile, 0.0)
    flat = jnp.sum(tile, axis=0, keepdims=True)[:, : batches * VALUES]
    for n in range(share_out.shape[0]):
        share_out[n] = flat


def relay_kernel(near, out):
    row = jnp.concatenate([near[n] for n in range(near.shape[0])], axis=1)
    for n in range(out.shape[0]):
        out[n] = row


def term_kernel(
    needed,
    shares,
    rho,
    weight,
    exchange_part,
    xyz,
    points_at,
    phi,
    inverse_far,
    multipoles_out,
    out,
    inverse,
    rows,
    spread,
    potential,
    total,
    load_sems,
):
    loads = [pltpu.make_async_copy(inverse_far.at[b], inverse.at[b], load_sems.at[b]) for b in range(phi.shape[0])]
    for load in loads:
        load.start()
    batches, points, width = phi.shape
    rel = width // 128
    devices = rows.shape[0]
    sources = shares.shape[0]
    each = batches * VALUES
    chunks = xyz.shape[1]

    rows[...] = jnp.zeros_like(rows)
    near = shares[...].reshape(sources, shares.shape[2])
    for g in range(devices // sources):
        rows[g * sources : (g + 1) * sources, :each] = near[:, g * each : (g + 1) * each]
    table = rows[...]
    turned = table.T
    low_at = lax.broadcasted_iota(jnp.int32, (devices, 128), 1).astype(F32)
    high_at = lax.broadcasted_iota(jnp.int32, (chunks, devices), 0).astype(F32)
    summed = jnp.zeros((12 * chunks, 128), F32)
    for b in range(batches):
        low = jnp.where(table[:, b * VALUES + 4 : b * VALUES + 5] == low_at, 1.0, 0.0).astype(BF16)
        high = jnp.where(turned[b * VALUES + 5 : b * VALUES + 6] == high_at, 1.0, 0.0)
        rest = turned[b * VALUES : (b + 1) * VALUES]
        stacked = []
        for _ in range(3):
            part = rest.astype(BF16).astype(F32)
            rest = rest - part
            stacked += [high * part[k : k + 1] for k in range(4)]
        stacked = jnp.concatenate(stacked, axis=0).astype(BF16)
        summed = summed + jnp.dot(stacked, low, preferred_element_type=F32)
    multipoles = [
        summed[k * chunks : (k + 1) * chunks]
        + (summed[(4 + k) * chunks : (5 + k) * chunks] + summed[(8 + k) * chunks : (9 + k) * chunks])
        for k in range(4)
    ]
    for k in range(4):
        multipoles_out[k * chunks : (k + 1) * chunks] = multipoles[k]
    shift = multipoles[1] * xyz[0] + multipoles[2] * xyz[1] + multipoles[3] * xyz[2]
    for k, value in enumerate(multipoles + [shift]):
        for h in range(chunks):
            spread[k * chunks + h] = jnp.broadcast_to(value[h : h + 1], (8, 128))

    filler = jnp.zeros((128 - 2 * batches, points), F32)
    features = jnp.concatenate([weight[...], exchange_part[...] * rho[...], filler], axis=0).T
    total[...] = jnp.zeros_like(total)
    rows_each = points // 8
    for b in range(batches):
        loads[b].wait()

        def potential_of(step, _, b=b):
            at = pl.ds(step * 8, 8)
            px, py, pz = (points_at[k, pl.ds(b * rows_each + step * 8, 8)] for k in range(3))
            acc = jnp.zeros((8, 8, 128), F32)
            for h in range(chunks):
                dipole = (
                    spread[chunks + h][None] * px
                    + spread[2 * chunks + h][None] * py
                    + spread[3 * chunks + h][None] * pz
                    - spread[4 * chunks + h][None]
                )
                s = inverse[b, h, at]
                acc = acc + s * (spread[h][None] + dipole * (s * s))
            potential[at] = acc
            return 0

        lax.fori_loop(0, rows_each // 8, potential_of, 0)
        hartree = jnp.sum(potential[...].reshape(points, 128), axis=1, keepdims=True)
        factor = features[:, b : b + 1] * (features[:, batches + b : batches + b + 1] + hartree)
        values = phi[b]
        scaled = (values.astype(F32) * factor).astype(BF16)
        for i in range(rel):
            term = lax.dot_general(
                scaled[:, i * 128 : (i + 1) * 128],
                values,
                (((0,), (0,)), ((), ())),
                preferred_element_type=F32,
            )
            for j in range(rel):
                q = needed[b, i * rel + j]
                total[q] += term[:, j * 128 : (j + 1) * 128]

    for w in range(8):
        for k in range(8):
            q = (k // 2) * 16 + w * 2 + k % 2
            for c in range(2):
                for y2 in range(2):
                    first = c * 64 + y2 * 32
                    out[(y2 * 2 + c) * 8 + w, k] = total[q, first : first + 32].astype(BF16)


def collect_kernel(asked, received, out, *totals):
    for total in totals:
        total[...] = jnp.zeros_like(total)
    w = lax.axis_index("z2") * 4 + lax.axis_index("x")

    def add_one(n, _):
        for k, total in enumerate(totals):
            total[asked_at(asked, n, w, k)] += received[n, k].astype(F32)
        return 0

    lax.fori_loop(0, received.shape[0], add_one, 0)
    for z4 in range(4):
        for h in range(4):
            two = [totals[2 * z4][2 * h + e] + totals[2 * z4 + 1][2 * h + e] for e in range(2)]
            for y4 in range(4):
                pair = jnp.concatenate([value[y4 * 8 : (y4 + 1) * 8] for value in two], axis=0)
                out[y4 * 4 + z4, h * 16 : (h + 1) * 16] = pair.astype(BF16)


def on_device(
    basis_values,
    stored_density_blocks,
    device_request,
    batch_blocks,
    batch_atom,
    point_offset,
    point_weight,
    exchange_kernel,
    atom_xyz,
):
    batches, points, width = basis_values.shape
    own, tile = stored_density_blocks.shape[0], stored_density_blocks.shape[1]
    atoms = atom_xyz.shape[1]
    padded = -(-atoms // 128) * 128
    part = tile // 4
    chunks = padded // 128
    each = batches * VALUES
    groups = batches * points // 8
    params = pltpu.CompilerParams(vmem_limit_bytes=32 * MIB)
    hbm = pl.BlockSpec(memory_space=pltpu.HBM)
    far_away = pl.BlockSpec(memory_space=pl.ANY)

    far = jnp.pad(atom_xyz, ((0, 0), (0, padded - atoms))).reshape(3, chunks, 128)
    points_at, inverse = pl.pallas_call(
        geometry_kernel,
        name="geometry",
        out_shape=(
            pltpu.VMEM((3, groups, 8, 128), F32),
            pltpu.HBM((batches, chunks, points // 8, 8, 128), F32),
        ),
        in_specs=smem(2) + vmem(2),
        out_specs=(vmem(1)[0], hbm),
        scratch_shapes=[
            pltpu.VMEM((batches, chunks, points // 8, 8, 128), F32),
            pltpu.SemaphoreType.DMA((batches,)),
        ],
        compiler_params=params,
        cost_estimate=pl.CostEstimate(flops=2 * 10**7, bytes_accessed=6 * MIB, transcendentals=10**6),
    )(batch_atom, atom_xyz, point_offset, far)

    message, slab = pl.pallas_call(
        prepare_kernel,
        name="prepare",
        out_shape=(pltpu.HBM((32, 1, 1024), jnp.int32), jax.ShapeDtypeStruct((own, part, tile), BF16)),
        in_specs=[hbm, hbm],
        out_specs=(hbm, vmem(1)[0]),
        scratch_shapes=[
            pltpu.VMEM((1, 2, 32), jnp.int32),
            pltpu.VMEM((32, 1, 1024), jnp.int32),
            pltpu.SemaphoreType.DMA((3,)),
        ],
        compiler_params=params,
    )(
        pltpu.with_memory_space_constraint(device_request.transpose(0, 2, 1), pltpu.HBM),
        pltpu.with_memory_space_constraint(stored_density_blocks, pltpu.HBM),
    )
    message = exchange(message, COLLECT)
    pieces = [slab] + [lax.ppermute(slab, "z4", [(i, (i + s) % 4) for i in range(4)]) for s in (1, 2, 3)]
    served, asked = pl.pallas_call(
        serve_kernel,
        name="serve",
        out_shape=(jax.ShapeDtypeStruct((32, 8, part, tile), BF16), jax.ShapeDtypeStruct((32, 1, 128), jnp.int32)),
        in_specs=[far_away] + vmem(4),
        out_specs=tuple(vmem(2)),
        scratch_shapes=[
            pltpu.SMEM((32, 1, 128), jnp.int32),
            pltpu.VMEM((4, own, part, tile), BF16),
            pltpu.SemaphoreType.DMA((2,)),
        ],
        compiler_params=params,
    )(message, *pieces)
    blocks = exchange(served, COLLECT)

    density, density_again, share = pl.pallas_call(
        density_kernel,
        name="density",
        out_shape=(
            jax.ShapeDtypeStruct((batches, points), F32),
            jax.ShapeDtypeStruct((batches, points), F32),
            jax.ShapeDtypeStruct((16, 1, each), F32),
        ),
        in_specs=smem(2) + vmem(4),
        out_specs=tuple(vmem(3)),
        scratch_shapes=[pltpu.VMEM((2, width, width), BF16)],
        compiler_params=params,
    )(batch_blocks, batch_atom, basis_values, blocks, point_weight, point_offset)

    shares = pl.pallas_call(
        relay_kernel,
        name="relay",
        out_shape=jax.ShapeDtypeStruct((32, 1, 16 * each), F32),
        in_specs=vmem(1),
        out_specs=vmem(1)[0],
        compiler_params=params,
    )(exchange(share, GRP))
    multipoles, outgoing = pl.pallas_call(
        term_kernel,
        name="terms",
        out_shape=(
            jax.ShapeDtypeStruct((4 * chunks, 128), F32),
            jax.ShapeDtypeStruct((32, 8, 32, tile), BF16),
        ),
        in_specs=smem(1) + vmem(7) + [hbm],
        out_specs=tuple(vmem(2)),
        scratch_shapes=[
            pltpu.VMEM(inverse.shape, F32),
            pltpu.VMEM((512, 128), F32),
            pltpu.VMEM((5 * chunks, 8, 128), F32),
            pltpu.VMEM((points // 8, 8, 128), F32),
            pltpu.VMEM((64, tile, tile), F32),
            pltpu.SemaphoreType.DMA((batches,)),
        ],
        compiler_params=params,
    )(
        batch_blocks,
        exchange(shares, DEV),
        density_again,
        point_weight,
        exchange_kernel,
        far,
        pltpu.with_memory_space_constraint(points_at, pltpu.VMEM),
        basis_values,
        pltpu.with_memory_space_constraint(inverse, pltpu.HBM),
    )

    received = exchange(outgoing, COLLECT)
    partial = pl.pallas_call(
        collect_kernel,
        name="collect",
        out_shape=jax.ShapeDtypeStruct((16, own * 8, tile), BF16),
        in_specs=smem(1) + vmem(1),
        out_specs=vmem(1)[0],
        scratch_shapes=[pltpu.VMEM((own, 32, tile), F32)] * 8,
        compiler_params=params,
    )(asked, received)
    settled = exchange(partial, SETTLE).astype(F32).sum(axis=0).astype(BF16)
    rows = exchange(jnp.broadcast_to(settled[None], (16, own * 8, tile)), GRP)
    rows = rows.reshape(4, 2, 2, own, 8, tile).transpose(3, 2, 1, 0, 4, 5)
    return (rows.reshape(own, tile, tile), density, multipoles.reshape(4, padded)[:, :atoms])


def solution(mesh):
    finer = Mesh(mesh.devices.reshape(4, 2, 2, 4, 2, 4), GRP_DEV)
    placed = (
        P(GRP_DEV, None, None),
        P(DEV, None, None),
        P(GRP_DEV, None, None),
        P(GRP_DEV, None),
        P(GRP_DEV),
        P(None, GRP_DEV, None),
        P(GRP_DEV, None),
        P(GRP_DEV, None),
        P(),
    )
    return jax.shard_map(
        on_device,
        mesh=finer,
        in_specs=placed,
        out_specs=(P(DEV, None, None), P(GRP_DEV, None), P()),
        check_vma=False,
    )
```

```python
import functools

import jax
import jax.numpy as jnp
from jax import lax
from jax.experimental import pallas as pl
from jax.experimental.pallas import tpu as pltpu
from jax.sharding import Mesh
from jax.sharding import PartitionSpec as P

GRP = ("y4", "y2", "c")
DEV = ("z4", "z2", "x")
GRP_DEV = GRP + DEV
COLLECT = ("y2", "c", "z2", "x")
SETTLE = ("y4", "z4")

F32 = jnp.float32
BF16 = jnp.bfloat16
MIB = 1024 * 1024
VALUES = 8


def exchange(value, axes):
    return lax.all_to_all(value, axes, split_axis=0, concat_axis=0, tiled=True)


def vmem(count):
    return [pl.BlockSpec(memory_space=pltpu.VMEM)] * count


def smem(count):
    return [pl.BlockSpec(memory_space=pltpu.SMEM)] * count


def place_of(position):
    return (position >> 1) & 7, (position >> 4) * 2 + (position & 1)


def prepare_kernel(request_far, stored, message, slab, request, staged, sems):
    ask = pltpu.make_async_copy(request_far, request, sems.at[2])
    ask.start()
    part = slab.shape[1]
    at = (lax.axis_index("c") * 2 + lax.axis_index("y2")) * part
    own = stored.at[:, pl.ds(pl.multiple_of(at, part), part)]
    load = pltpu.make_async_copy(own, slab, sems.at[0])
    load.start()
    slots, owners = request.shape[1], request.shape[2]
    ask.wait()
    flat = jnp.concatenate([request[0, k : k + 1] for k in range(slots)], axis=1)
    flat = jnp.concatenate([flat, jnp.zeros((1, staged.shape[2] - owners * slots), jnp.int32)], axis=1)
    for n in range(staged.shape[0]):
        staged[n] = flat
    save = pltpu.make_async_copy(staged, message, sems.at[1])
    save.start()
    save.wait()
    load.wait()


def asked_at(asked, n, w, k):
    return jnp.maximum(asked[n, 0, (k % 2) * 32 + (k // 2) * 8 + w], 0)


def serve_kernel(message, own, one, two, three, out, kept, asked, held, load_sems):
    few = message.at[:, :, pl.ds(0, 128)]
    loads = [pltpu.make_async_copy(few, target, load_sems.at[n]) for n, target in enumerate((asked, kept))]
    for load in loads:
        load.start()
    z4 = lax.axis_index("z4")
    w = lax.axis_index("z2") * 4 + lax.axis_index("x")
    for shift, piece in enumerate((own, one, two, three)):
        held[(z4 - shift) & 3] = piece[...]
    for load in loads:
        load.wait()
    for n in range(out.shape[0]):
        for k in range(8):
            out[n, k] = held[k // 2, asked_at(asked, n, w, k)]


def three_parts(value):
    parts = []
    for _ in range(3):
        parts.append(value.astype(BF16).astype(F32))
        value = value - parts[-1]
    return parts


def geometry_kernel(atom, places, offset, xyz, phi, left_out, turned_out, inverse_far, inverse, spots, sems):
    batches, points = offset.shape[1], offset.shape[2]
    chunks = xyz.shape[1]
    ones = jnp.ones((1, points), F32)
    filler = jnp.zeros((128 - 24, points), F32)
    copies = []
    for b in range(batches):
        spot = [offset[k, b : b + 1] + places[k, atom[b]] for k in range(3)] + [ones]
        spot = jnp.concatenate(spot, axis=0)
        high, middle, low = three_parts(spot)
        stacked = jnp.concatenate([high, high, middle, high, low, middle, filler], axis=0)
        left_out[b] = stacked.T.astype(BF16)
        turned_out[b] = phi[b].T
        columns = jnp.concatenate([spot, jnp.zeros((124, points), F32)], axis=0).T
        for k in range(3):
            spots[k] = jnp.broadcast_to(columns[:, k : k + 1], (points, 128))

        def inverse_of(step, _, b=b):
            at = pl.ds(step * 64, 64)
            px, py, pz = (spots[k, at] for k in range(3))
            for h in range(chunks):
                gx = px - xyz[0, h : h + 1]
                gy = py - xyz[1, h : h + 1]
                gz = pz - xyz[2, h : h + 1]
                inverse[b, h, at] = lax.rsqrt(gx * gx + gy * gy + gz * gz + 1.0)
            return 0

        lax.fori_loop(0, points // 64, inverse_of, 0)
        copies.append(pltpu.make_async_copy(inverse.at[b], inverse_far.at[b], sems.at[b]))
        copies[-1].start()
    for copy in copies:
        copy.wait()


def density_kernel(needed, atom, phi, blocks, weight, offset, rho_out, rho_again, share_out, wide):
    batches, points, width = phi.shape
    rel = width // 128
    part = blocks.shape[2]
    lane = lax.broadcasted_iota(jnp.int32, (points, 128), 1)
    columns = jnp.zeros((points, 128), F32)
    for b in range(batches):
        for p in range(rel * rel):
            w, k = place_of(needed[b, p])
            i, j = p // rel, p % rel
            for c in range(2):
                for y2 in range(2):
                    at = i * 128 + (c * 2 + y2) * part
                    wide[b % 2, pl.ds(at, part), pl.ds(j * 128, 128)] = blocks[(y2 * 2 + c) * 8 + w, k]
        values = phi[b]
        product = jnp.dot(values, wide[b % 2], preferred_element_type=F32) * values.astype(F32)
        folded = product[:, :128]
        for j in range(1, rel):
            folded = folded + product[:, j * 128 : (j + 1) * 128]
        columns = jnp.where(lane == b, jnp.sum(folded, axis=1, keepdims=True), columns)
    rho = columns.T[:batches]
    rho_out[...] = rho
    rho_again[...] = rho
    weighted = rho * weight[...]
    moments = [weighted] + [weighted * offset[k] for k in range(3)]
    spot = lax.broadcasted_iota(jnp.int32, (batches, 128), 1)
    row = lax.broadcasted_iota(jnp.int32, (batches, 128), 0)
    tile = jnp.zeros((batches, 128), F32)
    for k, moment in enumerate(moments):
        tile = jnp.where(spot % VALUES == k, jnp.sum(moment, axis=1, keepdims=True), tile)
    for b in range(batches):
        mine = row == b
        tile = jnp.where((spot % VALUES == 4) & mine, (atom[b] & 127).astype(F32), tile)
        tile = jnp.where((spot % VALUES == 5) & mine, (atom[b] >> 7).astype(F32), tile)
    tile = jnp.where(spot // VALUES == row, tile, 0.0)
    flat = jnp.sum(tile, axis=0, keepdims=True)[:, : batches * VALUES]
    for n in range(share_out.shape[0]):
        share_out[n] = flat


def relay_kernel(near, out):
    row = jnp.concatenate([near[n] for n in range(near.shape[0])], axis=1)
    for n in range(out.shape[0]):
        out[n] = row


def term_kernel(
    needed,
    shares,
    rho,
    weight,
    exchange_part,
    xyz,
    left,
    turned_phi,
    phi,
    inverse_far,
    multipoles_out,
    out,
    inverse,
    rows,
    right,
    total,
    load_sems,
):
    batches, points, width = phi.shape
    loads = [pltpu.make_async_copy(inverse_far.at[b], inverse.at[b], load_sems.at[b]) for b in range(batches)]
    for load in loads:
        load.start()
    rel = width // 128
    devices = rows.shape[0]
    sources = shares.shape[0]
    each = batches * VALUES
    chunks = xyz.shape[1]
    atoms = multipoles_out.shape[1]

    rows[...] = jnp.zeros_like(rows)
    near = shares[...].reshape(sources, shares.shape[2])
    for g in range(devices // sources):
        rows[g * sources : (g + 1) * sources, :each] = near[:, g * each : (g + 1) * each]
    table = rows[...]
    turned = table.T
    low_at = lax.broadcasted_iota(jnp.int32, (devices, 128), 1).astype(F32)
    high_at = lax.broadcasted_iota(jnp.int32, (chunks, devices), 0).astype(F32)
    summed = jnp.zeros((12 * chunks, 128), F32)
    for b in range(batches):
        low = jnp.where(table[:, b * VALUES + 4 : b * VALUES + 5] == low_at, 1.0, 0.0).astype(BF16)
        high = jnp.where(turned[b * VALUES + 5 : b * VALUES + 6] == high_at, 1.0, 0.0)
        stacked = []
        for piece in three_parts(turned[b * VALUES : (b + 1) * VALUES]):
            stacked += [high * piece[k : k + 1] for k in range(4)]
        stacked = jnp.concatenate(stacked, axis=0).astype(BF16)
        summed = summed + jnp.dot(stacked, low, preferred_element_type=F32)
    multipoles = [
        summed[k * chunks : (k + 1) * chunks]
        + (summed[(4 + k) * chunks : (5 + k) * chunks] + summed[(8 + k) * chunks : (9 + k) * chunks])
        for k in range(4)
    ]
    for k in range(4):
        for h in range(chunks):
            count = min(128, atoms - h * 128)
            multipoles_out[k : k + 1, h * 128 : h * 128 + count] = multipoles[k][h : h + 1, :count]

    shift = multipoles[1] * xyz[0] + multipoles[2] * xyz[1] + multipoles[3] * xyz[2]
    parts = [three_parts(value) for value in (multipoles[1], multipoles[2], multipoles[3], -shift)]
    right[...] = jnp.zeros_like(right)
    for h in range(chunks):
        stacked = [parts[k][n][h : h + 1] for n in (0, 1, 0, 2, 0, 1) for k in range(4)]
        stacked = jnp.concatenate(stacked + [jnp.zeros((8, 128), F32)], axis=0)
        right[:32, h * 128 : (h + 1) * 128] = stacked.astype(BF16)

    total[...] = jnp.zeros_like(total)
    for b in range(batches):
        dipole = jnp.dot(left[b], right[...], preferred_element_type=F32)
        loads[b].wait()
        acc = jnp.zeros((points, 128), F32)
        for h in range(chunks):
            s = inverse[b, h]
            acc = acc + s * (multipoles[0][h : h + 1] + dipole[:, h * 128 : (h + 1) * 128] * (s * s))
        hartree = jnp.sum(acc.T, axis=0, keepdims=True)
        factor = weight[b : b + 1] * (exchange_part[b : b + 1] * rho[b : b + 1] + hartree)
        scaled = (turned_phi[b].astype(F32) * factor).astype(BF16)
        for i in range(rel):
            term = jnp.dot(scaled[i * 128 : (i + 1) * 128], phi[b], preferred_element_type=F32)
            for j in range(rel):
                q = needed[b, i * rel + j]
                total[q] += term[:, j * 128 : (j + 1) * 128]

    for w in range(8):
        for k in range(8):
            q = (k // 2) * 16 + w * 2 + k % 2
            for c in range(2):
                for y2 in range(2):
                    first = c * 64 + y2 * 32
                    out[(y2 * 2 + c) * 8 + w, k] = total[q, first : first + 32].astype(BF16)


def collect_kernel(asked, received, out, *totals):
    for total in totals:
        total[...] = jnp.zeros_like(total)
    w = lax.axis_index("z2") * 4 + lax.axis_index("x")

    def add_one(n, _):
        for k, total in enumerate(totals):
            total[asked_at(asked, n, w, k)] += received[n, k].astype(F32)
        return 0

    lax.fori_loop(0, received.shape[0], add_one, 0)
    for z4 in range(4):
        for h in range(4):
            two = [totals[2 * z4][2 * h + e] + totals[2 * z4 + 1][2 * h + e] for e in range(2)]
            for y4 in range(4):
                pair = jnp.concatenate([value[y4 * 8 : (y4 + 1) * 8] for value in two], axis=0)
                out[y4 * 4 + z4, h * 16 : (h + 1) * 16] = pair.astype(BF16)


def settle_kernel(received, out):
    summed = received[0].astype(F32)
    for n in range(1, received.shape[0]):
        summed = summed + received[n].astype(F32)
    summed = summed.astype(BF16)
    for n in range(out.shape[0]):
        out[n] = summed


def on_device(
    basis_values,
    stored_density_blocks,
    device_request,
    batch_blocks,
    batch_atom,
    point_offset,
    point_weight,
    exchange_kernel,
    atom_xyz,
):
    batches, points, width = basis_values.shape
    own, tile = stored_density_blocks.shape[0], stored_density_blocks.shape[1]
    atoms = atom_xyz.shape[1]
    padded = -(-atoms // 128) * 128
    part = tile // 4
    chunks = padded // 128
    each = batches * VALUES
    params = pltpu.CompilerParams(vmem_limit_bytes=32 * MIB)
    hbm = pl.BlockSpec(memory_space=pltpu.HBM)
    anywhere = pl.BlockSpec(memory_space=pl.ANY)

    far = jnp.pad(atom_xyz, ((0, 0), (0, padded - atoms))).reshape(3, chunks, 128)
    left, turned_phi, inverse = pl.pallas_call(
        geometry_kernel,
        name="geometry",
        out_shape=(
            jax.ShapeDtypeStruct((batches, points, 128), BF16),
            jax.ShapeDtypeStruct((batches, width, points), BF16),
            pltpu.HBM((batches, chunks, points, 128), F32),
        ),
        in_specs=smem(2) + vmem(3),
        out_specs=tuple(vmem(2)) + (hbm,),
        scratch_shapes=[
            pltpu.VMEM((batches, chunks, points, 128), F32),
            pltpu.VMEM((3, points, 128), F32),
            pltpu.SemaphoreType.DMA((batches,)),
        ],
        compiler_params=params,
        cost_estimate=pl.CostEstimate(flops=2 * 10**7, bytes_accessed=6 * MIB, transcendentals=10**6),
    )(batch_atom, atom_xyz, point_offset, far, basis_values)

    message, slab = pl.pallas_call(
        prepare_kernel,
        name="prepare",
        out_shape=(pltpu.HBM((32, 1, 1024), jnp.int32), jax.ShapeDtypeStruct((own, part, tile), BF16)),
        in_specs=[hbm, hbm],
        out_specs=(hbm, vmem(1)[0]),
        scratch_shapes=[
            pltpu.VMEM((1, 2, 32), jnp.int32),
            pltpu.VMEM((32, 1, 1024), jnp.int32),
            pltpu.SemaphoreType.DMA((3,)),
        ],
        compiler_params=params,
    )(
        pltpu.with_memory_space_constraint(device_request.transpose(0, 2, 1), pltpu.HBM),
        pltpu.with_memory_space_constraint(stored_density_blocks, pltpu.HBM),
    )
    message = exchange(message, COLLECT)
    pieces = [slab] + [lax.ppermute(slab, "z4", [(i, (i + s) % 4) for i in range(4)]) for s in (1, 2, 3)]
    served, asked = pl.pallas_call(
        serve_kernel,
        name="serve",
        out_shape=(jax.ShapeDtypeStruct((32, 8, part, tile), BF16), jax.ShapeDtypeStruct((32, 1, 128), jnp.int32)),
        in_specs=[anywhere] + vmem(4),
        out_specs=tuple(vmem(2)),
        scratch_shapes=[
            pltpu.SMEM((32, 1, 128), jnp.int32),
            pltpu.VMEM((4, own, part, tile), BF16),
            pltpu.SemaphoreType.DMA((2,)),
        ],
        compiler_params=params,
    )(message, *pieces)
    blocks = exchange(served, COLLECT)

    density, density_again, share = pl.pallas_call(
        density_kernel,
        name="density",
        out_shape=(
            jax.ShapeDtypeStruct((batches, points), F32),
            jax.ShapeDtypeStruct((batches, points), F32),
            jax.ShapeDtypeStruct((16, 1, each), F32),
        ),
        in_specs=smem(2) + vmem(4),
        out_specs=tuple(vmem(3)),
        scratch_shapes=[pltpu.VMEM((2, width, width), BF16)],
        compiler_params=params,
    )(batch_blocks, batch_atom, basis_values, blocks, point_weight, point_offset)

    shares = pl.pallas_call(
        relay_kernel,
        name="relay",
        out_shape=jax.ShapeDtypeStruct((32, 1, 16 * each), F32),
        in_specs=vmem(1),
        out_specs=vmem(1)[0],
        compiler_params=params,
    )(exchange(share, GRP))
    multipoles, outgoing = pl.pallas_call(
        term_kernel,
        name="terms",
        out_shape=(
            jax.ShapeDtypeStruct((4, atoms), F32),
            jax.ShapeDtypeStruct((32, 8, 32, tile), BF16),
        ),
        in_specs=smem(1) + vmem(8) + [hbm],
        out_specs=tuple(vmem(2)),
        scratch_shapes=[
            pltpu.VMEM(inverse.shape, F32),
            pltpu.VMEM((512, 128), F32),
            pltpu.VMEM((128, padded), BF16),
            pltpu.VMEM((64, tile, tile), F32),
            pltpu.SemaphoreType.DMA((batches,)),
        ],
        compiler_params=params,
    )(
        batch_blocks,
        exchange(shares, DEV),
        density_again,
        point_weight,
        exchange_kernel,
        far,
        left,
        turned_phi,
        basis_values,
        pltpu.with_memory_space_constraint(inverse, pltpu.HBM),
    )

    received = exchange(outgoing, COLLECT)
    partial = pl.pallas_call(
        collect_kernel,
        name="collect",
        out_shape=jax.ShapeDtypeStruct((16, own * 8, tile), BF16),
        in_specs=smem(1) + vmem(1),
        out_specs=vmem(1)[0],
        scratch_shapes=[pltpu.VMEM((own, 32, tile), F32)] * 8,
        compiler_params=params,
    )(asked, received)
    settled = pl.pallas_call(
        settle_kernel,
        name="settle",
        out_shape=jax.ShapeDtypeStruct((16, own * 8, tile), BF16),
        in_specs=vmem(1),
        out_specs=vmem(1)[0],
        compiler_params=params,
    )(exchange(partial, SETTLE))
    rows = exchange(settled, GRP)
    rows = rows.reshape(4, 2, 2, own, 8, tile).transpose(3, 2, 1, 0, 4, 5)
    return (rows.reshape(own, tile, tile), density, multipoles)


def solution(mesh):
    finer = Mesh(mesh.devices.reshape(4, 2, 2, 4, 2, 4), GRP_DEV)
    placed = (
        P(GRP_DEV, None, None),
        P(DEV, None, None),
        P(GRP_DEV, None, None),
        P(GRP_DEV, None),
        P(GRP_DEV),
        P(None, GRP_DEV, None),
        P(GRP_DEV, None),
        P(GRP_DEV, None),
        P(),
    )
    return jax.shard_map(
        on_device,
        mesh=finer,
        in_specs=placed,
        out_specs=(P(DEV, None, None), P(GRP_DEV, None), P()),
        check_vma=False,
    )
```

```python
import functools

import jax
import jax.numpy as jnp
from jax import lax
from jax.experimental import pallas as pl
from jax.experimental.pallas import tpu as pltpu
from jax.sharding import Mesh
from jax.sharding import PartitionSpec as P

GRP = ("y4", "y2", "c")
DEV = ("z4", "z2", "x")
GRP_DEV = GRP + DEV
COLLECT = ("y2", "c", "z2", "x")
SETTLE = ("y4", "z4")

F32 = jnp.float32
BF16 = jnp.bfloat16
MIB = 1024 * 1024
VALUES = 8


def exchange(value, axes):
    return lax.all_to_all(value, axes, split_axis=0, concat_axis=0, tiled=True)


def vmem(count):
    return [pl.BlockSpec(memory_space=pltpu.VMEM)] * count


def smem(count):
    return [pl.BlockSpec(memory_space=pltpu.SMEM)] * count


def place_of(position):
    return (position >> 1) & 7, (position >> 4) * 2 + (position & 1)


def prepare_kernel(request_far, stored, message, slab, request, staged, sems):
    ask = pltpu.make_async_copy(request_far, request, sems.at[2])
    ask.start()
    part = slab.shape[1]
    at = (lax.axis_index("c") * 2 + lax.axis_index("y2")) * part
    own = stored.at[:, pl.ds(pl.multiple_of(at, part), part)]
    load = pltpu.make_async_copy(own, slab, sems.at[0])
    load.start()
    slots, owners = request.shape[1], request.shape[2]
    ask.wait()
    flat = jnp.concatenate([request[0, k : k + 1] for k in range(slots)], axis=1)
    flat = jnp.concatenate([flat, jnp.zeros((1, staged.shape[2] - owners * slots), jnp.int32)], axis=1)
    for n in range(staged.shape[0]):
        staged[n] = flat
    save = pltpu.make_async_copy(staged, message, sems.at[1])
    save.start()
    save.wait()
    load.wait()


def asked_at(asked, n, w, k):
    return jnp.maximum(asked[n, 0, (k % 2) * 32 + (k // 2) * 8 + w], 0)


def serve_kernel(message, held, out, kept, asked, load_sems):
    few = message.at[:, :, pl.ds(0, 128)]
    loads = [pltpu.make_async_copy(few, target, load_sems.at[n]) for n, target in enumerate((asked, kept))]
    for load in loads:
        load.start()
    w = lax.axis_index("z2") * 4 + lax.axis_index("x")
    for load in loads:
        load.wait()
    for n in range(out.shape[0]):
        for k in range(8):
            out[n, k] = held[(k // 2) * 8 + asked_at(asked, n, w, k)]


def three_parts(value):
    parts = []
    for _ in range(3):
        parts.append(value.astype(BF16).astype(F32))
        value = value - parts[-1]
    return parts


def geometry_kernel(atom, places, offset, xyz, phi, left_out, turned_out, inverse_far, inverse, spots, sems):
    batches, points = offset.shape[1], offset.shape[2]
    chunks = xyz.shape[1]
    ones = jnp.ones((1, points), F32)
    filler = jnp.zeros((128 - 24, points), F32)
    copies = []
    for b in range(batches):
        spot = [offset[k, b : b + 1] + places[k, atom[b]] for k in range(3)] + [ones]
        spot = jnp.concatenate(spot, axis=0)
        high, middle, low = three_parts(spot)
        stacked = jnp.concatenate([high, high, middle, high, low, middle, filler], axis=0)
        left_out[b] = stacked.T.astype(BF16)
        turned_out[b] = phi[b].T
        columns = jnp.concatenate([spot, jnp.zeros((124, points), F32)], axis=0).T
        for k in range(3):
            spots[k] = jnp.broadcast_to(columns[:, k : k + 1], (points, 128))

        def inverse_of(step, _, b=b):
            at = pl.ds(step * 64, 64)
            px, py, pz = (spots[k, at] for k in range(3))
            for h in range(chunks):
                gx = px - xyz[0, h : h + 1]
                gy = py - xyz[1, h : h + 1]
                gz = pz - xyz[2, h : h + 1]
                inverse[b, h, at] = lax.rsqrt(gx * gx + gy * gy + gz * gz + 1.0)
            return 0

        lax.fori_loop(0, points // 64, inverse_of, 0)
        copies.append(pltpu.make_async_copy(inverse.at[b], inverse_far.at[b], sems.at[b]))
        copies[-1].start()
    for copy in copies:
        copy.wait()


def density_kernel(needed, atom, phi, blocks, weight, offset, rho_out, rho_again, share_out, wide):
    batches, points, width = phi.shape
    rel = width // 128
    part = blocks.shape[2]
    lane = lax.broadcasted_iota(jnp.int32, (points, 128), 1)
    columns = jnp.zeros((points, 128), F32)
    for b in range(batches):
        for p in range(rel * rel):
            w, k = place_of(needed[b, p])
            i, j = p // rel, p % rel
            for c in range(2):
                for y2 in range(2):
                    at = i * 128 + (c * 2 + y2) * part
                    wide[b % 2, pl.ds(at, part), pl.ds(j * 128, 128)] = blocks[(y2 * 2 + c) * 8 + w, k]
        values = phi[b]
        product = jnp.dot(values, wide[b % 2], preferred_element_type=F32) * values.astype(F32)
        folded = product[:, :128]
        for j in range(1, rel):
            folded = folded + product[:, j * 128 : (j + 1) * 128]
        columns = jnp.where(lane == b, jnp.sum(folded, axis=1, keepdims=True), columns)
    rho = columns.T[:batches]
    rho_out[...] = rho
    rho_again[...] = rho
    weighted = rho * weight[...]
    moments = [weighted] + [weighted * offset[k] for k in range(3)]
    spot = lax.broadcasted_iota(jnp.int32, (batches, 128), 1)
    row = lax.broadcasted_iota(jnp.int32, (batches, 128), 0)
    tile = jnp.zeros((batches, 128), F32)
    for k, moment in enumerate(moments):
        tile = jnp.where(spot % VALUES == k, jnp.sum(moment, axis=1, keepdims=True), tile)
    for b in range(batches):
        mine = row == b
        tile = jnp.where((spot % VALUES == 4) & mine, (atom[b] & 127).astype(F32), tile)
        tile = jnp.where((spot % VALUES == 5) & mine, (atom[b] >> 7).astype(F32), tile)
    tile = jnp.where(spot // VALUES == row, tile, 0.0)
    flat = jnp.sum(tile, axis=0, keepdims=True)[:, : batches * VALUES]
    for n in range(share_out.shape[0]):
        share_out[n] = flat


def relay_kernel(near, out):
    row = jnp.concatenate([near[n] for n in range(near.shape[0])], axis=1)
    for n in range(out.shape[0]):
        out[n] = row


def term_kernel(
    needed,
    shares,
    rho,
    weight,
    exchange_part,
    xyz,
    left,
    turned_phi,
    phi,
    inverse_far,
    multipoles_out,
    out,
    inverse,
    rows,
    right,
    total,
    load_sems,
):
    batches, points, width = phi.shape
    loads = [pltpu.make_async_copy(inverse_far.at[b], inverse.at[b], load_sems.at[b]) for b in range(batches)]
    for load in loads:
        load.start()
    rel = width // 128
    devices = rows.shape[0]
    sources = shares.shape[0]
    each = batches * VALUES
    chunks = xyz.shape[1]
    atoms = multipoles_out.shape[1]

    rows[...] = jnp.zeros_like(rows)
    near = shares[...].reshape(sources, shares.shape[2])
    for g in range(devices // sources):
        rows[g * sources : (g + 1) * sources, :each] = near[:, g * each : (g + 1) * each]
    table = rows[...]
    turned = table.T
    low_at = lax.broadcasted_iota(jnp.int32, (devices, 128), 1).astype(F32)
    high_at = lax.broadcasted_iota(jnp.int32, (chunks, devices), 0).astype(F32)
    summed = jnp.zeros((12 * chunks, 128), F32)
    for b in range(batches):
        low = jnp.where(table[:, b * VALUES + 4 : b * VALUES + 5] == low_at, 1.0, 0.0).astype(BF16)
        high = jnp.where(turned[b * VALUES + 5 : b * VALUES + 6] == high_at, 1.0, 0.0)
        stacked = []
        for piece in three_parts(turned[b * VALUES : (b + 1) * VALUES]):
            stacked += [high * piece[k : k + 1] for k in range(4)]
        stacked = jnp.concatenate(stacked, axis=0).astype(BF16)
        summed = summed + jnp.dot(stacked, low, preferred_element_type=F32)
    multipoles = [
        summed[k * chunks : (k + 1) * chunks]
        + (summed[(4 + k) * chunks : (5 + k) * chunks] + summed[(8 + k) * chunks : (9 + k) * chunks])
        for k in range(4)
    ]
    for k in range(4):
        for h in range(chunks):
            count = min(128, atoms - h * 128)
            multipoles_out[k : k + 1, h * 128 : h * 128 + count] = multipoles[k][h : h + 1, :count]

    shift = multipoles[1] * xyz[0] + multipoles[2] * xyz[1] + multipoles[3] * xyz[2]
    parts = [three_parts(value) for value in (multipoles[1], multipoles[2], multipoles[3], -shift)]
    right[...] = jnp.zeros_like(right)
    for h in range(chunks):
        stacked = [parts[k][n][h : h + 1] for n in (0, 1, 0, 2, 0, 1) for k in range(4)]
        stacked = jnp.concatenate(stacked + [jnp.zeros((8, 128), F32)], axis=0)
        right[:32, h * 128 : (h + 1) * 128] = stacked.astype(BF16)

    total[...] = jnp.zeros_like(total)
    for b in range(batches):
        dipole = jnp.dot(left[b], right[...], preferred_element_type=F32)
        loads[b].wait()
        acc = jnp.zeros((points, 128), F32)
        for h in range(chunks):
            s = inverse[b, h]
            acc = acc + s * (multipoles[0][h : h + 1] + dipole[:, h * 128 : (h + 1) * 128] * (s * s))
        hartree = jnp.sum(acc.T, axis=0, keepdims=True)
        factor = weight[b : b + 1] * (exchange_part[b : b + 1] * rho[b : b + 1] + hartree)
        scaled = (turned_phi[b].astype(F32) * factor).astype(BF16)
        for i in range(rel):
            term = jnp.dot(scaled[i * 128 : (i + 1) * 128], phi[b], preferred_element_type=F32)
            for j in range(rel):
                q = needed[b, i * rel + j]
                total[q] += term[:, j * 128 : (j + 1) * 128]

    for w in range(8):
        for k in range(8):
            q = (k // 2) * 16 + w * 2 + k % 2
            for c in range(2):
                for y2 in range(2):
                    first = c * 64 + y2 * 32
                    out[(y2 * 2 + c) * 8 + w, k] = total[q, first : first + 32].astype(BF16)


def collect_kernel(asked, received, out, *totals):
    for total in totals:
        total[...] = jnp.zeros_like(total)
    w = lax.axis_index("z2") * 4 + lax.axis_index("x")

    def add_one(n, _):
        for k, total in enumerate(totals):
            total[asked_at(asked, n, w, k)] += received[n, k].astype(F32)
        return 0

    lax.fori_loop(0, received.shape[0], add_one, 0)
    for z4 in range(4):
        for h in range(4):
            two = [totals[2 * z4][2 * h + e] + totals[2 * z4 + 1][2 * h + e] for e in range(2)]
            for y4 in range(4):
                pair = jnp.concatenate([value[y4 * 8 : (y4 + 1) * 8] for value in two], axis=0)
                out[y4 * 4 + z4, h * 16 : (h + 1) * 16] = pair.astype(BF16)


def settle_kernel(received, out):
    summed = received[0].astype(F32)
    for n in range(1, received.shape[0]):
        summed = summed + received[n].astype(F32)
    summed = summed.astype(BF16)
    for n in range(out.shape[0]):
        out[n] = summed


def on_device(
    basis_values,
    stored_density_blocks,
    device_request,
    batch_blocks,
    batch_atom,
    point_offset,
    point_weight,
    exchange_kernel,
    atom_xyz,
):
    batches, points, width = basis_values.shape
    own, tile = stored_density_blocks.shape[0], stored_density_blocks.shape[1]
    atoms = atom_xyz.shape[1]
    padded = -(-atoms // 128) * 128
    part = tile // 4
    chunks = padded // 128
    each = batches * VALUES
    params = pltpu.CompilerParams(vmem_limit_bytes=32 * MIB)
    hbm = pl.BlockSpec(memory_space=pltpu.HBM)
    anywhere = pl.BlockSpec(memory_space=pl.ANY)

    far = jnp.pad(atom_xyz, ((0, 0), (0, padded - atoms))).reshape(3, chunks, 128)
    left, turned_phi, inverse = pl.pallas_call(
        geometry_kernel,
        name="geometry",
        out_shape=(
            jax.ShapeDtypeStruct((batches, points, 128), BF16),
            jax.ShapeDtypeStruct((batches, width, points), BF16),
            pltpu.HBM((batches, chunks, points, 128), F32),
        ),
        in_specs=smem(2) + vmem(3),
        out_specs=tuple(vmem(2)) + (hbm,),
        scratch_shapes=[
            pltpu.VMEM((batches, chunks, points, 128), F32),
            pltpu.VMEM((3, points, 128), F32),
            pltpu.SemaphoreType.DMA((batches,)),
        ],
        compiler_params=params,
        cost_estimate=pl.CostEstimate(flops=2 * 10**7, bytes_accessed=6 * MIB, transcendentals=10**6),
    )(batch_atom, atom_xyz, point_offset, far, basis_values)

    message, slab = pl.pallas_call(
        prepare_kernel,
        name="prepare",
        out_shape=(pltpu.HBM((32, 1, 128), jnp.int32), jax.ShapeDtypeStruct((own, part, tile), BF16)),
        in_specs=[hbm, hbm],
        out_specs=(hbm, vmem(1)[0]),
        scratch_shapes=[
            pltpu.VMEM((1, 2, 32), jnp.int32),
            pltpu.VMEM((32, 1, 128), jnp.int32),
            pltpu.SemaphoreType.DMA((3,)),
        ],
        compiler_params=params,
    )(
        pltpu.with_memory_space_constraint(device_request.transpose(0, 2, 1), pltpu.HBM),
        pltpu.with_memory_space_constraint(stored_density_blocks, pltpu.HBM),
    )
    message = exchange(message, COLLECT)
    pieces = lax.all_gather(slab, "z4", tiled=True)
    served, asked = pl.pallas_call(
        serve_kernel,
        name="serve",
        out_shape=(jax.ShapeDtypeStruct((32, 8, part, tile), BF16), jax.ShapeDtypeStruct((32, 1, 128), jnp.int32)),
        in_specs=[anywhere] + vmem(1),
        out_specs=tuple(vmem(2)),
        scratch_shapes=[
            pltpu.SMEM((32, 1, 128), jnp.int32),
            pltpu.SemaphoreType.DMA((2,)),
        ],
        compiler_params=params,
    )(message, pieces)
    blocks = exchange(served, COLLECT)

    density, density_again, share = pl.pallas_call(
        density_kernel,
        name="density",
        out_shape=(
            jax.ShapeDtypeStruct((batches, points), F32),
            jax.ShapeDtypeStruct((batches, points), F32),
            jax.ShapeDtypeStruct((16, 1, each), F32),
        ),
        in_specs=smem(2) + vmem(4),
        out_specs=tuple(vmem(3)),
        scratch_shapes=[pltpu.VMEM((2, width, width), BF16)],
        compiler_params=params,
    )(batch_blocks, batch_atom, basis_values, blocks, point_weight, point_offset)

    shares = pl.pallas_call(
        relay_kernel,
        name="relay",
        out_shape=jax.ShapeDtypeStruct((32, 1, 16 * each), F32),
        in_specs=vmem(1),
        out_specs=vmem(1)[0],
        compiler_params=params,
    )(exchange(share, GRP))
    multipoles, outgoing = pl.pallas_call(
        term_kernel,
        name="terms",
        out_shape=(
            jax.ShapeDtypeStruct((4, atoms), F32),
            jax.ShapeDtypeStruct((32, 8, 32, tile), BF16),
        ),
        in_specs=smem(1) + vmem(8) + [hbm],
        out_specs=tuple(vmem(2)),
        scratch_shapes=[
            pltpu.VMEM(inverse.shape, F32),
            pltpu.VMEM((512, 128), F32),
            pltpu.VMEM((128, padded), BF16),
            pltpu.VMEM((64, tile, tile), F32),
            pltpu.SemaphoreType.DMA((batches,)),
        ],
        compiler_params=params,
    )(
        batch_blocks,
        exchange(shares, DEV),
        density_again,
        point_weight,
        exchange_kernel,
        far,
        left,
        turned_phi,
        basis_values,
        pltpu.with_memory_space_constraint(inverse, pltpu.HBM),
    )

    received = exchange(outgoing, COLLECT)
    partial = pl.pallas_call(
        collect_kernel,
        name="collect",
        out_shape=jax.ShapeDtypeStruct((16, own * 8, tile), BF16),
        in_specs=smem(1) + vmem(1),
        out_specs=vmem(1)[0],
        scratch_shapes=[pltpu.VMEM((own, 32, tile), F32)] * 8,
        compiler_params=params,
    )(asked, received)
    settled = pl.pallas_call(
        settle_kernel,
        name="settle",
        out_shape=jax.ShapeDtypeStruct((16, own * 8, tile), BF16),
        in_specs=vmem(1),
        out_specs=vmem(1)[0],
        compiler_params=params,
    )(exchange(partial, SETTLE))
    rows = exchange(settled, GRP)
    rows = rows.reshape(4, 2, 2, own, 8, tile).transpose(3, 2, 1, 0, 4, 5)
    return (rows.reshape(own, tile, tile), density, multipoles)


def solution(mesh):
    finer = Mesh(mesh.devices.reshape(4, 2, 2, 4, 2, 4), GRP_DEV)
    placed = (
        P(GRP_DEV, None, None),
        P(DEV, None, None),
        P(GRP_DEV, None, None),
        P(GRP_DEV, None),
        P(GRP_DEV),
        P(None, GRP_DEV, None),
        P(GRP_DEV, None),
        P(GRP_DEV, None),
        P(),
    )
    return jax.shard_map(
        on_device,
        mesh=finer,
        in_specs=placed,
        out_specs=(P(DEV, None, None), P(GRP_DEV, None), P()),
        check_vma=False,
    )
```

```python
import functools

import jax
import jax.numpy as jnp
from jax import lax
from jax.experimental import pallas as pl
from jax.experimental.pallas import tpu as pltpu
from jax.sharding import Mesh
from jax.sharding import PartitionSpec as P

GRP = ("y4", "y2", "c")
DEV = ("z4", "z2", "x")
GRP_DEV = GRP + DEV
COLLECT = ("y2", "c", "z2", "x")
SETTLE = ("y4", "z4")
NEAR = ("c", "x")
FAR = ("y4", "y2", "z4", "z2")

F32 = jnp.float32
BF16 = jnp.bfloat16
MIB = 1024 * 1024
VALUES = 8


def exchange(value, axes):
    return lax.all_to_all(value, axes, split_axis=0, concat_axis=0, tiled=True)


def vmem(count):
    return [pl.BlockSpec(memory_space=pltpu.VMEM)] * count


def smem(count):
    return [pl.BlockSpec(memory_space=pltpu.SMEM)] * count


def place_of(position):
    return (position >> 1) & 7, (position >> 4) * 2 + (position & 1)


def prepare_kernel(request_far, stored, message, slab, request, staged, sems):
    ask = pltpu.make_async_copy(request_far, request, sems.at[2])
    ask.start()
    part = slab.shape[1]
    at = (lax.axis_index("c") * 2 + lax.axis_index("y2")) * part
    own = stored.at[:, pl.ds(pl.multiple_of(at, part), part)]
    load = pltpu.make_async_copy(own, slab, sems.at[0])
    load.start()
    slots, owners = request.shape[1], request.shape[2]
    ask.wait()
    flat = jnp.concatenate([request[0, k : k + 1] for k in range(slots)], axis=1)
    flat = jnp.concatenate([flat, jnp.zeros((1, staged.shape[2] - owners * slots), jnp.int32)], axis=1)
    for n in range(staged.shape[0]):
        staged[n] = flat
    save = pltpu.make_async_copy(staged, message, sems.at[1])
    save.start()
    save.wait()
    load.wait()


def asked_at(asked, n, w, k):
    return jnp.maximum(asked[n, 0, (k % 2) * 32 + (k // 2) * 8 + w], 0)


def serve_kernel(message, held, out, kept, asked, load_sems):
    few = message.at[:, :, pl.ds(0, 128)]
    loads = [pltpu.make_async_copy(few, target, load_sems.at[n]) for n, target in enumerate((asked, kept))]
    for load in loads:
        load.start()
    w = lax.axis_index("z2") * 4 + lax.axis_index("x")
    for load in loads:
        load.wait()
    for n in range(out.shape[0]):
        for k in range(8):
            out[n, k] = held[(k // 2) * 8 + asked_at(asked, n, w, k)]


def three_parts(value):
    parts = []
    for _ in range(3):
        parts.append(value.astype(BF16).astype(F32))
        value = value - parts[-1]
    return parts


def geometry_kernel(atom, places, offset, xyz, phi, left_out, turned_out, inverse_far, inverse, spots, sems):
    batches, points = offset.shape[1], offset.shape[2]
    chunks = xyz.shape[1]
    ones = jnp.ones((1, points), F32)
    filler = jnp.zeros((128 - 24, points), F32)
    copies = []
    for b in range(batches):
        spot = [offset[k, b : b + 1] + places[k, atom[b]] for k in range(3)] + [ones]
        spot = jnp.concatenate(spot, axis=0)
        high, middle, low = three_parts(spot)
        stacked = jnp.concatenate([high, high, middle, high, low, middle, filler], axis=0)
        left_out[b] = stacked.T.astype(BF16)
        turned_out[b] = phi[b].T
        columns = jnp.concatenate([spot, jnp.zeros((124, points), F32)], axis=0).T
        for k in range(3):
            spots[k] = jnp.broadcast_to(columns[:, k : k + 1], (points, 128))

        def inverse_of(step, _, b=b):
            at = pl.ds(step * 64, 64)
            px, py, pz = (spots[k, at] for k in range(3))
            for h in range(chunks):
                gx = px - xyz[0, h : h + 1]
                gy = py - xyz[1, h : h + 1]
                gz = pz - xyz[2, h : h + 1]
                inverse[b, h, at] = lax.rsqrt(gx * gx + gy * gy + gz * gz + 1.0)
            return 0

        lax.fori_loop(0, points // 64, inverse_of, 0)
        copies.append(pltpu.make_async_copy(inverse.at[b], inverse_far.at[b], sems.at[b]))
        copies[-1].start()
    for copy in copies:
        copy.wait()


def density_kernel(needed, atom, phi, blocks, weight, offset, rho_out, rho_again, share_out, wide):
    batches, points, width = phi.shape
    rel = width // 128
    part = blocks.shape[2]
    lane = lax.broadcasted_iota(jnp.int32, (points, 128), 1)
    columns = jnp.zeros((points, 128), F32)
    for b in range(batches):
        for p in range(rel * rel):
            w, k = place_of(needed[b, p])
            i, j = p // rel, p % rel
            for c in range(2):
                for y2 in range(2):
                    at = i * 128 + (c * 2 + y2) * part
                    wide[b % 2, pl.ds(at, part), pl.ds(j * 128, 128)] = blocks[(y2 * 2 + c) * 8 + w, k]
        values = phi[b]
        product = jnp.dot(values, wide[b % 2], preferred_element_type=F32) * values.astype(F32)
        folded = product[:, :128]
        for j in range(1, rel):
            folded = folded + product[:, j * 128 : (j + 1) * 128]
        columns = jnp.where(lane == b, jnp.sum(folded, axis=1, keepdims=True), columns)
    rho = columns.T[:batches]
    rho_out[...] = rho
    rho_again[...] = rho
    weighted = rho * weight[...]
    moments = [weighted] + [weighted * offset[k] for k in range(3)]
    spot = lax.broadcasted_iota(jnp.int32, (batches, 128), 1)
    row = lax.broadcasted_iota(jnp.int32, (batches, 128), 0)
    tile = jnp.zeros((batches, 128), F32)
    for k, moment in enumerate(moments):
        tile = jnp.where(spot % VALUES == k, jnp.sum(moment, axis=1, keepdims=True), tile)
    for b in range(batches):
        mine = row == b
        tile = jnp.where((spot % VALUES == 4) & mine, (atom[b] & 127).astype(F32), tile)
        tile = jnp.where((spot % VALUES == 5) & mine, (atom[b] >> 7).astype(F32), tile)
    tile = jnp.where(spot // VALUES == row, tile, 0.0)
    flat = jnp.sum(tile, axis=0, keepdims=True)[:, : batches * VALUES]
    for n in range(share_out.shape[0]):
        share_out[n] = flat


def relay_kernel(near, out):
    row = jnp.concatenate([near[n] for n in range(near.shape[0])], axis=1)
    for n in range(out.shape[0]):
        out[n] = row


def term_kernel(
    needed,
    shares,
    rho,
    weight,
    exchange_part,
    xyz,
    left,
    turned_phi,
    phi,
    inverse_far,
    multipoles_out,
    out,
    inverse,
    rows,
    right,
    total,
    load_sems,
):
    batches, points, width = phi.shape
    loads = [pltpu.make_async_copy(inverse_far.at[b], inverse.at[b], load_sems.at[b]) for b in range(batches)]
    for load in loads:
        load.start()
    rel = width // 128
    devices = rows.shape[0]
    sources = shares.shape[0]
    each = batches * VALUES
    chunks = xyz.shape[1]
    atoms = multipoles_out.shape[1]

    rows[...] = jnp.zeros_like(rows)
    near = shares[...].reshape(sources, shares.shape[2])
    for g in range(devices // sources):
        rows[g * sources : (g + 1) * sources, :each] = near[:, g * each : (g + 1) * each]
    table = rows[...]
    turned = table.T
    low_at = lax.broadcasted_iota(jnp.int32, (devices, 128), 1).astype(F32)
    high_at = lax.broadcasted_iota(jnp.int32, (chunks, devices), 0).astype(F32)
    summed = jnp.zeros((12 * chunks, 128), F32)
    for b in range(batches):
        low = jnp.where(table[:, b * VALUES + 4 : b * VALUES + 5] == low_at, 1.0, 0.0).astype(BF16)
        high = jnp.where(turned[b * VALUES + 5 : b * VALUES + 6] == high_at, 1.0, 0.0)
        stacked = []
        for piece in three_parts(turned[b * VALUES : (b + 1) * VALUES]):
            stacked += [high * piece[k : k + 1] for k in range(4)]
        stacked = jnp.concatenate(stacked, axis=0).astype(BF16)
        summed = summed + jnp.dot(stacked, low, preferred_element_type=F32)
    multipoles = [
        summed[k * chunks : (k + 1) * chunks]
        + (summed[(4 + k) * chunks : (5 + k) * chunks] + summed[(8 + k) * chunks : (9 + k) * chunks])
        for k in range(4)
    ]
    for k in range(4):
        for h in range(chunks):
            count = min(128, atoms - h * 128)
            multipoles_out[k : k + 1, h * 128 : h * 128 + count] = multipoles[k][h : h + 1, :count]

    shift = multipoles[1] * xyz[0] + multipoles[2] * xyz[1] + multipoles[3] * xyz[2]
    parts = [three_parts(value) for value in (multipoles[1], multipoles[2], multipoles[3], -shift)]
    right[...] = jnp.zeros_like(right)
    for h in range(chunks):
        stacked = [parts[k][n][h : h + 1] for n in (0, 1, 0, 2, 0, 1) for k in range(4)]
        stacked = jnp.concatenate(stacked + [jnp.zeros((8, 128), F32)], axis=0)
        right[:32, h * 128 : (h + 1) * 128] = stacked.astype(BF16)

    total[...] = jnp.zeros_like(total)
    for b in range(batches):
        dipole = jnp.dot(left[b], right[...], preferred_element_type=F32)
        loads[b].wait()
        acc = jnp.zeros((points, 128), F32)
        for h in range(chunks):
            s = inverse[b, h]
            acc = acc + s * (multipoles[0][h : h + 1] + dipole[:, h * 128 : (h + 1) * 128] * (s * s))
        hartree = jnp.sum(acc.T, axis=0, keepdims=True)
        factor = weight[b : b + 1] * (exchange_part[b : b + 1] * rho[b : b + 1] + hartree)
        scaled = (turned_phi[b].astype(F32) * factor).astype(BF16)
        for i in range(rel):
            term = jnp.dot(scaled[i * 128 : (i + 1) * 128], phi[b], preferred_element_type=F32)
            for j in range(rel):
                q = needed[b, i * rel + j]
                total[q] += term[:, j * 128 : (j + 1) * 128]

    for w in range(8):
        for k in range(8):
            q = (k // 2) * 16 + w * 2 + k % 2
            for c in range(2):
                for y2 in range(2):
                    first = c * 64 + y2 * 32
                    out[(y2 * 2 + c) * 8 + w, k] = total[q, first : first + 32].astype(BF16)


def collect_kernel(asked, received, out, *totals):
    for total in totals:
        total[...] = jnp.zeros_like(total)
    w = lax.axis_index("z2") * 4 + lax.axis_index("x")

    def add_one(n, _):
        for k, total in enumerate(totals):
            total[asked_at(asked, n, w, k)] += received[n, k].astype(F32)
        return 0

    lax.fori_loop(0, received.shape[0], add_one, 0)
    for z4 in range(4):
        for h in range(4):
            two = [totals[2 * z4][2 * h + e] + totals[2 * z4 + 1][2 * h + e] for e in range(2)]
            for y4 in range(4):
                pair = jnp.concatenate([value[y4 * 8 : (y4 + 1) * 8] for value in two], axis=0)
                out[y4 * 4 + z4, h * 16 : (h + 1) * 16] = pair.astype(BF16)


def settle_kernel(received, out):
    summed = received[0].astype(F32)
    for n in range(1, received.shape[0]):
        summed = summed + received[n].astype(F32)
    summed = summed.astype(BF16)
    for n in range(out.shape[0]):
        out[n] = summed


def on_device(
    basis_values,
    stored_density_blocks,
    device_request,
    batch_blocks,
    batch_atom,
    point_offset,
    point_weight,
    exchange_kernel,
    atom_xyz,
):
    batches, points, width = basis_values.shape
    own, tile = stored_density_blocks.shape[0], stored_density_blocks.shape[1]
    atoms = atom_xyz.shape[1]
    padded = -(-atoms // 128) * 128
    part = tile // 4
    chunks = padded // 128
    each = batches * VALUES
    params = pltpu.CompilerParams(vmem_limit_bytes=32 * MIB)
    hbm = pl.BlockSpec(memory_space=pltpu.HBM)
    anywhere = pl.BlockSpec(memory_space=pl.ANY)

    far = jnp.pad(atom_xyz, ((0, 0), (0, padded - atoms))).reshape(3, chunks, 128)
    left, turned_phi, inverse = pl.pallas_call(
        geometry_kernel,
        name="geometry",
        out_shape=(
            jax.ShapeDtypeStruct((batches, points, 128), BF16),
            jax.ShapeDtypeStruct((batches, width, points), BF16),
            pltpu.HBM((batches, chunks, points, 128), F32),
        ),
        in_specs=smem(2) + vmem(3),
        out_specs=tuple(vmem(2)) + (hbm,),
        scratch_shapes=[
            pltpu.VMEM((batches, chunks, points, 128), F32),
            pltpu.VMEM((3, points, 128), F32),
            pltpu.SemaphoreType.DMA((batches,)),
        ],
        compiler_params=params,
        cost_estimate=pl.CostEstimate(flops=2 * 10**7, bytes_accessed=6 * MIB, transcendentals=10**6),
    )(batch_atom, atom_xyz, point_offset, far, basis_values)

    message, slab = pl.pallas_call(
        prepare_kernel,
        name="prepare",
        out_shape=(pltpu.HBM((32, 1, 128), jnp.int32), jax.ShapeDtypeStruct((own, part, tile), BF16)),
        in_specs=[hbm, hbm],
        out_specs=(hbm, vmem(1)[0]),
        scratch_shapes=[
            pltpu.VMEM((1, 2, 32), jnp.int32),
            pltpu.VMEM((32, 1, 128), jnp.int32),
            pltpu.SemaphoreType.DMA((3,)),
        ],
        compiler_params=params,
    )(
        pltpu.with_memory_space_constraint(device_request.transpose(0, 2, 1), pltpu.HBM),
        pltpu.with_memory_space_constraint(stored_density_blocks, pltpu.HBM),
    )
    message = exchange(message, COLLECT)
    pieces = lax.all_gather(slab, "z4", tiled=True)
    served, asked = pl.pallas_call(
        serve_kernel,
        name="serve",
        out_shape=(jax.ShapeDtypeStruct((32, 8, part, tile), BF16), jax.ShapeDtypeStruct((32, 1, 128), jnp.int32)),
        in_specs=[anywhere] + vmem(1),
        out_specs=tuple(vmem(2)),
        scratch_shapes=[
            pltpu.SMEM((32, 1, 128), jnp.int32),
            pltpu.SemaphoreType.DMA((2,)),
        ],
        compiler_params=params,
    )(message, pieces)
    blocks = exchange(served, COLLECT)

    density, density_again, share = pl.pallas_call(
        density_kernel,
        name="density",
        out_shape=(
            jax.ShapeDtypeStruct((batches, points), F32),
            jax.ShapeDtypeStruct((batches, points), F32),
            jax.ShapeDtypeStruct((8, 1, each), F32),
        ),
        in_specs=smem(2) + vmem(4),
        out_specs=tuple(vmem(3)),
        scratch_shapes=[pltpu.VMEM((2, width, width), BF16)],
        compiler_params=params,
    )(batch_blocks, batch_atom, basis_values, blocks, point_weight, point_offset)

    shares = pl.pallas_call(
        relay_kernel,
        name="relay",
        out_shape=jax.ShapeDtypeStruct((64, 1, 8 * each), F32),
        in_specs=vmem(1),
        out_specs=vmem(1)[0],
        compiler_params=params,
    )(exchange(share, NEAR))
    multipoles, outgoing = pl.pallas_call(
        term_kernel,
        name="terms",
        out_shape=(
            jax.ShapeDtypeStruct((4, atoms), F32),
            jax.ShapeDtypeStruct((32, 8, 32, tile), BF16),
        ),
        in_specs=smem(1) + vmem(8) + [hbm],
        out_specs=tuple(vmem(2)),
        scratch_shapes=[
            pltpu.VMEM(inverse.shape, F32),
            pltpu.VMEM((512, 128), F32),
            pltpu.VMEM((128, padded), BF16),
            pltpu.VMEM((64, tile, tile), F32),
            pltpu.SemaphoreType.DMA((batches,)),
        ],
        compiler_params=params,
    )(
        batch_blocks,
        exchange(shares, FAR),
        density_again,
        point_weight,
        exchange_kernel,
        far,
        left,
        turned_phi,
        basis_values,
        pltpu.with_memory_space_constraint(inverse, pltpu.HBM),
    )

    received = exchange(outgoing, COLLECT)
    partial = pl.pallas_call(
        collect_kernel,
        name="collect",
        out_shape=jax.ShapeDtypeStruct((16, own * 8, tile), BF16),
        in_specs=smem(1) + vmem(1),
        out_specs=vmem(1)[0],
        scratch_shapes=[pltpu.VMEM((own, 32, tile), F32)] * 8,
        compiler_params=params,
    )(asked, received)
    settled = pl.pallas_call(
        settle_kernel,
        name="settle",
        out_shape=jax.ShapeDtypeStruct((16, own * 8, tile), BF16),
        in_specs=vmem(1),
        out_specs=vmem(1)[0],
        compiler_params=params,
    )(exchange(partial, SETTLE))
    rows = exchange(settled, GRP)
    rows = rows.reshape(4, 2, 2, own, 8, tile).transpose(3, 2, 1, 0, 4, 5)
    return (rows.reshape(own, tile, tile), density, multipoles)


def solution(mesh):
    finer = Mesh(mesh.devices.reshape(4, 2, 2, 4, 2, 4), GRP_DEV)
    placed = (
        P(GRP_DEV, None, None),
        P(DEV, None, None),
        P(GRP_DEV, None, None),
        P(GRP_DEV, None),
        P(GRP_DEV),
        P(None, GRP_DEV, None),
        P(GRP_DEV, None),
        P(GRP_DEV, None),
        P(),
    )
    return jax.shard_map(
        on_device,
        mesh=finer,
        in_specs=placed,
        out_specs=(P(DEV, None, None), P(GRP_DEV, None), P()),
        check_vma=False,
    )
```

```python
import functools

import jax
import jax.numpy as jnp
from jax import lax
from jax.experimental import pallas as pl
from jax.experimental.pallas import tpu as pltpu
from jax.sharding import Mesh
from jax.sharding import PartitionSpec as P

GRP = ("y4", "y2", "c")
DEV = ("z4", "z2", "x")
GRP_DEV = GRP + DEV
SERVE = ("c", "z2", "x")
COLLECT = ("y2", "c", "z2", "x")
SETTLE = ("y4", "z4")
NEAR = ("c", "x")
FAR = ("y4", "y2", "z4", "z2")

F32 = jnp.float32
BF16 = jnp.bfloat16
MIB = 1024 * 1024
VALUES = 8


def exchange(value, axes):
    return lax.all_to_all(value, axes, split_axis=0, concat_axis=0, tiled=True)


def vmem(count):
    return [pl.BlockSpec(memory_space=pltpu.VMEM)] * count


def smem(count):
    return [pl.BlockSpec(memory_space=pltpu.SMEM)] * count


def place_of(position):
    return (position >> 1) & 7, (position >> 4) * 2 + (position & 1)


def prepare_kernel(request_far, stored, message, slab, request, staged, sems):
    ask = pltpu.make_async_copy(request_far, request, sems.at[2])
    ask.start()
    part = slab.shape[1]
    at = lax.axis_index("c") * part
    own = stored.at[:, pl.ds(pl.multiple_of(at, part), part)]
    load = pltpu.make_async_copy(own, slab, sems.at[0])
    load.start()
    slots, owners = request.shape[1], request.shape[2]
    ask.wait()
    flat = jnp.concatenate([request[0, k : k + 1] for k in range(slots)], axis=1)
    flat = jnp.concatenate([flat, jnp.zeros((1, staged.shape[2] - owners * slots), jnp.int32)], axis=1)
    for n in range(staged.shape[0]):
        staged[n] = flat
    save = pltpu.make_async_copy(staged, message, sems.at[1])
    save.start()
    save.wait()
    load.wait()


def asked_at(asked, n, w, k):
    return jnp.maximum(asked[n, 0, (k % 2) * 32 + (k // 2) * 8 + w], 0)


def serve_kernel(asked, held, out):
    w = lax.axis_index("z2") * 4 + lax.axis_index("x")
    first = lax.axis_index("y2") * out.shape[0]
    for n in range(out.shape[0]):
        for k in range(8):
            out[n, k] = held[(k // 2) * 8 + asked_at(asked, first + n, w, k)]


def three_parts(value):
    parts = []
    for _ in range(3):
        parts.append(value.astype(BF16).astype(F32))
        value = value - parts[-1]
    return parts


def geometry_kernel(atom, places, offset, xyz, phi, left_out, turned_out, inverse_far, inverse, spots, sems):
    batches, points = offset.shape[1], offset.shape[2]
    chunks = xyz.shape[1]
    ones = jnp.ones((1, points), F32)
    filler = jnp.zeros((128 - 24, points), F32)
    copies = []
    for b in range(batches):
        spot = [offset[k, b : b + 1] + places[k, atom[b]] for k in range(3)] + [ones]
        spot = jnp.concatenate(spot, axis=0)
        high, middle, low = three_parts(spot)
        stacked = jnp.concatenate([high, high, middle, high, low, middle, filler], axis=0)
        left_out[b] = stacked.T.astype(BF16)
        turned_out[b] = phi[b].T
        columns = jnp.concatenate([spot, jnp.zeros((124, points), F32)], axis=0).T
        for k in range(3):
            spots[k] = jnp.broadcast_to(columns[:, k : k + 1], (points, 128))

        def inverse_of(step, _, b=b):
            at = pl.ds(step * 64, 64)
            px, py, pz = (spots[k, at] for k in range(3))
            for h in range(chunks):
                gx = px - xyz[0, h : h + 1]
                gy = py - xyz[1, h : h + 1]
                gz = pz - xyz[2, h : h + 1]
                inverse[b, h, at] = lax.rsqrt(gx * gx + gy * gy + gz * gz + 1.0)
            return 0

        lax.fori_loop(0, points // 64, inverse_of, 0)
        copies.append(pltpu.make_async_copy(inverse.at[b], inverse_far.at[b], sems.at[b]))
        copies[-1].start()
    for copy in copies:
        copy.wait()


def density_kernel(needed, atom, phi, blocks, weight, offset, rho_out, rho_again, share_out, wide):
    batches, points, width = phi.shape
    rel = width // 128
    part = blocks.shape[2]
    lane = lax.broadcasted_iota(jnp.int32, (points, 128), 1)
    columns = jnp.zeros((points, 128), F32)
    for b in range(batches):
        for p in range(rel * rel):
            w, k = place_of(needed[b, p])
            i, j = p // rel, p % rel
            for c in range(2):
                at = i * 128 + c * part
                wide[b % 2, pl.ds(at, part), pl.ds(j * 128, 128)] = blocks[c * 8 + w, k]
        values = phi[b]
        product = jnp.dot(values, wide[b % 2], preferred_element_type=F32) * values.astype(F32)
        folded = product[:, :128]
        for j in range(1, rel):
            folded = folded + product[:, j * 128 : (j + 1) * 128]
        columns = jnp.where(lane == b, jnp.sum(folded, axis=1, keepdims=True), columns)
    rho = columns.T[:batches]
    rho_out[...] = rho
    rho_again[...] = rho
    weighted = rho * weight[...]
    moments = [weighted] + [weighted * offset[k] for k in range(3)]
    spot = lax.broadcasted_iota(jnp.int32, (batches, 128), 1)
    row = lax.broadcasted_iota(jnp.int32, (batches, 128), 0)
    tile = jnp.zeros((batches, 128), F32)
    for k, moment in enumerate(moments):
        tile = jnp.where(spot % VALUES == k, jnp.sum(moment, axis=1, keepdims=True), tile)
    for b in range(batches):
        mine = row == b
        tile = jnp.where((spot % VALUES == 4) & mine, (atom[b] & 127).astype(F32), tile)
        tile = jnp.where((spot % VALUES == 5) & mine, (atom[b] >> 7).astype(F32), tile)
    tile = jnp.where(spot // VALUES == row, tile, 0.0)
    flat = jnp.sum(tile, axis=0, keepdims=True)[:, : batches * VALUES]
    for n in range(share_out.shape[0]):
        share_out[n] = flat


def relay_kernel(near, out):
    row = jnp.concatenate([near[n] for n in range(near.shape[0])], axis=1)
    for n in range(out.shape[0]):
        out[n] = row


def term_kernel(
    needed,
    shares,
    rho,
    weight,
    exchange_part,
    xyz,
    left,
    turned_phi,
    phi,
    inverse_far,
    multipoles_out,
    out,
    inverse,
    rows,
    right,
    total,
    load_sems,
):
    batches, points, width = phi.shape
    loads = [pltpu.make_async_copy(inverse_far.at[b], inverse.at[b], load_sems.at[b]) for b in range(batches)]
    for load in loads:
        load.start()
    rel = width // 128
    devices = rows.shape[0]
    sources = shares.shape[0]
    each = batches * VALUES
    chunks = xyz.shape[1]
    atoms = multipoles_out.shape[1]

    rows[...] = jnp.zeros_like(rows)
    near = shares[...].reshape(sources, shares.shape[2])
    for g in range(devices // sources):
        rows[g * sources : (g + 1) * sources, :each] = near[:, g * each : (g + 1) * each]
    table = rows[...]
    turned = table.T
    low_at = lax.broadcasted_iota(jnp.int32, (devices, 128), 1).astype(F32)
    high_at = lax.broadcasted_iota(jnp.int32, (chunks, devices), 0).astype(F32)
    summed = jnp.zeros((12 * chunks, 128), F32)
    for b in range(batches):
        low = jnp.where(table[:, b * VALUES + 4 : b * VALUES + 5] == low_at, 1.0, 0.0).astype(BF16)
        high = jnp.where(turned[b * VALUES + 5 : b * VALUES + 6] == high_at, 1.0, 0.0)
        stacked = []
        for piece in three_parts(turned[b * VALUES : (b + 1) * VALUES]):
            stacked += [high * piece[k : k + 1] for k in range(4)]
        stacked = jnp.concatenate(stacked, axis=0).astype(BF16)
        summed = summed + jnp.dot(stacked, low, preferred_element_type=F32)
    multipoles = [
        summed[k * chunks : (k + 1) * chunks]
        + (summed[(4 + k) * chunks : (5 + k) * chunks] + summed[(8 + k) * chunks : (9 + k) * chunks])
        for k in range(4)
    ]
    for k in range(4):
        for h in range(chunks):
            count = min(128, atoms - h * 128)
            multipoles_out[k : k + 1, h * 128 : h * 128 + count] = multipoles[k][h : h + 1, :count]

    shift = multipoles[1] * xyz[0] + multipoles[2] * xyz[1] + multipoles[3] * xyz[2]
    parts = [three_parts(value) for value in (multipoles[1], multipoles[2], multipoles[3], -shift)]
    right[...] = jnp.zeros_like(right)
    for h in range(chunks):
        stacked = [parts[k][n][h : h + 1] for n in (0, 1, 0, 2, 0, 1) for k in range(4)]
        stacked = jnp.concatenate(stacked + [jnp.zeros((8, 128), F32)], axis=0)
        right[:32, h * 128 : (h + 1) * 128] = stacked.astype(BF16)

    total[...] = jnp.zeros_like(total)
    for b in range(batches):
        dipole = jnp.dot(left[b], right[...], preferred_element_type=F32)
        loads[b].wait()
        acc = jnp.zeros((points, 128), F32)
        for h in range(chunks):
            s = inverse[b, h]
            acc = acc + s * (multipoles[0][h : h + 1] + dipole[:, h * 128 : (h + 1) * 128] * (s * s))
        hartree = jnp.sum(acc.T, axis=0, keepdims=True)
        factor = weight[b : b + 1] * (exchange_part[b : b + 1] * rho[b : b + 1] + hartree)
        scaled = (turned_phi[b].astype(F32) * factor).astype(BF16)
        for i in range(rel):
            term = jnp.dot(scaled[i * 128 : (i + 1) * 128], phi[b], preferred_element_type=F32)
            for j in range(rel):
                q = needed[b, i * rel + j]
                total[q] += term[:, j * 128 : (j + 1) * 128]

    for w in range(8):
        for k in range(8):
            q = (k // 2) * 16 + w * 2 + k % 2
            for c in range(2):
                for y2 in range(2):
                    first = c * 64 + y2 * 32
                    out[(y2 * 2 + c) * 8 + w, k] = total[q, first : first + 32].astype(BF16)


def collect_kernel(asked, received, out, *totals):
    for total in totals:
        total[...] = jnp.zeros_like(total)
    w = lax.axis_index("z2") * 4 + lax.axis_index("x")

    def add_one(n, _):
        for k, total in enumerate(totals):
            total[asked_at(asked, n, w, k)] += received[n, k].astype(F32)
        return 0

    lax.fori_loop(0, received.shape[0], add_one, 0)
    for z4 in range(4):
        for h in range(4):
            two = [totals[2 * z4][2 * h + e] + totals[2 * z4 + 1][2 * h + e] for e in range(2)]
            for y4 in range(4):
                pair = jnp.concatenate([value[y4 * 8 : (y4 + 1) * 8] for value in two], axis=0)
                out[y4 * 4 + z4, h * 16 : (h + 1) * 16] = pair.astype(BF16)


def settle_kernel(received, out):
    summed = received[0].astype(F32)
    for n in range(1, received.shape[0]):
        summed = summed + received[n].astype(F32)
    summed = summed.astype(BF16)
    for n in range(out.shape[0]):
        out[n] = summed


def on_device(
    basis_values,
    stored_density_blocks,
    device_request,
    batch_blocks,
    batch_atom,
    point_offset,
    point_weight,
    exchange_kernel,
    atom_xyz,
):
    batches, points, width = basis_values.shape
    own, tile = stored_density_blocks.shape[0], stored_density_blocks.shape[1]
    atoms = atom_xyz.shape[1]
    padded = -(-atoms // 128) * 128
    part = tile // 2
    chunks = padded // 128
    each = batches * VALUES
    params = pltpu.CompilerParams(vmem_limit_bytes=32 * MIB)
    hbm = pl.BlockSpec(memory_space=pltpu.HBM)

    far = jnp.pad(atom_xyz, ((0, 0), (0, padded - atoms))).reshape(3, chunks, 128)
    left, turned_phi, inverse = pl.pallas_call(
        geometry_kernel,
        name="geometry",
        out_shape=(
            jax.ShapeDtypeStruct((batches, points, 128), BF16),
            jax.ShapeDtypeStruct((batches, width, points), BF16),
            pltpu.HBM((batches, chunks, points, 128), F32),
        ),
        in_specs=smem(2) + vmem(3),
        out_specs=tuple(vmem(2)) + (hbm,),
        scratch_shapes=[
            pltpu.VMEM((batches, chunks, points, 128), F32),
            pltpu.VMEM((3, points, 128), F32),
            pltpu.SemaphoreType.DMA((batches,)),
        ],
        compiler_params=params,
        cost_estimate=pl.CostEstimate(flops=2 * 10**7, bytes_accessed=6 * MIB, transcendentals=10**6),
    )(batch_atom, atom_xyz, point_offset, far, basis_values)

    message, slab = pl.pallas_call(
        prepare_kernel,
        name="prepare",
        out_shape=(pltpu.HBM((32, 1, 128), jnp.int32), jax.ShapeDtypeStruct((own, part, tile), BF16)),
        in_specs=[hbm, hbm],
        out_specs=(hbm, vmem(1)[0]),
        scratch_shapes=[
            pltpu.VMEM((1, 2, 32), jnp.int32),
            pltpu.VMEM((32, 1, 128), jnp.int32),
            pltpu.SemaphoreType.DMA((3,)),
        ],
        compiler_params=params,
    )(
        pltpu.with_memory_space_constraint(device_request.transpose(0, 2, 1), pltpu.HBM),
        pltpu.with_memory_space_constraint(stored_density_blocks, pltpu.HBM),
    )
    asked = exchange(message, COLLECT)
    pieces = lax.all_gather(slab, "z4", tiled=True)
    served = pl.pallas_call(
        serve_kernel,
        name="serve",
        out_shape=jax.ShapeDtypeStruct((16, 8, part, tile), BF16),
        in_specs=smem(1) + vmem(1),
        out_specs=vmem(1)[0],
        compiler_params=params,
    )(asked, pieces)
    blocks = exchange(served, SERVE)

    density, density_again, share = pl.pallas_call(
        density_kernel,
        name="density",
        out_shape=(
            jax.ShapeDtypeStruct((batches, points), F32),
            jax.ShapeDtypeStruct((batches, points), F32),
            jax.ShapeDtypeStruct((8, 1, each), F32),
        ),
        in_specs=smem(2) + vmem(4),
        out_specs=tuple(vmem(3)),
        scratch_shapes=[pltpu.VMEM((2, width, width), BF16)],
        compiler_params=params,
    )(batch_blocks, batch_atom, basis_values, blocks, point_weight, point_offset)

    shares = pl.pallas_call(
        relay_kernel,
        name="relay",
        out_shape=jax.ShapeDtypeStruct((64, 1, 8 * each), F32),
        in_specs=vmem(1),
        out_specs=vmem(1)[0],
        compiler_params=params,
    )(exchange(share, NEAR))
    multipoles, outgoing = pl.pallas_call(
        term_kernel,
        name="terms",
        out_shape=(
            jax.ShapeDtypeStruct((4, atoms), F32),
            jax.ShapeDtypeStruct((32, 8, 32, tile), BF16),
        ),
        in_specs=smem(1) + vmem(8) + [hbm],
        out_specs=tuple(vmem(2)),
        scratch_shapes=[
            pltpu.VMEM(inverse.shape, F32),
            pltpu.VMEM((512, 128), F32),
            pltpu.VMEM((128, padded), BF16),
            pltpu.VMEM((64, tile, tile), F32),
            pltpu.SemaphoreType.DMA((batches,)),
        ],
        compiler_params=params,
    )(
        batch_blocks,
        exchange(shares, FAR),
        density_again,
        point_weight,
        exchange_kernel,
        far,
        left,
        turned_phi,
        basis_values,
        pltpu.with_memory_space_constraint(inverse, pltpu.HBM),
    )

    received = exchange(outgoing, COLLECT)
    partial = pl.pallas_call(
        collect_kernel,
        name="collect",
        out_shape=jax.ShapeDtypeStruct((16, own * 8, tile), BF16),
        in_specs=smem(1) + vmem(1),
        out_specs=vmem(1)[0],
        scratch_shapes=[pltpu.VMEM((own, 32, tile), F32)] * 8,
        compiler_params=params,
    )(asked, received)
    settled = pl.pallas_call(
        settle_kernel,
        name="settle",
        out_shape=jax.ShapeDtypeStruct((16, own * 8, tile), BF16),
        in_specs=vmem(1),
        out_specs=vmem(1)[0],
        compiler_params=params,
    )(exchange(partial, SETTLE))
    rows = exchange(settled, GRP)
    rows = rows.reshape(4, 2, 2, own, 8, tile).transpose(3, 2, 1, 0, 4, 5)
    return (rows.reshape(own, tile, tile), density, multipoles)


def solution(mesh):
    finer = Mesh(mesh.devices.reshape(4, 2, 2, 4, 2, 4), GRP_DEV)
    placed = (
        P(GRP_DEV, None, None),
        P(DEV, None, None),
        P(GRP_DEV, None, None),
        P(GRP_DEV, None),
        P(GRP_DEV),
        P(None, GRP_DEV, None),
        P(GRP_DEV, None),
        P(GRP_DEV, None),
        P(),
    )
    return jax.shard_map(
        on_device,
        mesh=finer,
        in_specs=placed,
        out_specs=(P(DEV, None, None), P(GRP_DEV, None), P()),
        check_vma=False,
    )
```

```python
import functools

import jax
import jax.numpy as jnp
from jax import lax
from jax.experimental import pallas as pl
from jax.experimental.pallas import tpu as pltpu
from jax.sharding import Mesh
from jax.sharding import PartitionSpec as P

GRP = ("y4", "y2", "c")
DEV = ("z4", "z2", "x")
GRP_DEV = GRP + DEV
COLLECT = ("y2", "c", "z2", "x")
SETTLE = ("y4", "z4")
NEAR = ("c", "x")
FAR = ("y4", "y2", "z4", "z2")

F32 = jnp.float32
BF16 = jnp.bfloat16
MIB = 1024 * 1024
VALUES = 8


def exchange(value, axes):
    return lax.all_to_all(value, axes, split_axis=0, concat_axis=0, tiled=True)


def vmem(count):
    return [pl.BlockSpec(memory_space=pltpu.VMEM)] * count


def smem(count):
    return [pl.BlockSpec(memory_space=pltpu.SMEM)] * count


def place_of(position):
    return (position >> 1) & 7, (position >> 4) * 2 + (position & 1)


def prepare_kernel(request_far, stored, message, slab, request, staged, sems):
    ask = pltpu.make_async_copy(request_far, request, sems.at[2])
    ask.start()
    part = slab.shape[1]
    at = (lax.axis_index("c") * 2 + lax.axis_index("y2")) * part
    own = stored.at[:, pl.ds(pl.multiple_of(at, part), part)]
    load = pltpu.make_async_copy(own, slab, sems.at[0])
    load.start()
    slots, owners = request.shape[1], request.shape[2]
    ask.wait()
    flat = jnp.concatenate([request[0, k : k + 1] for k in range(slots)], axis=1)
    flat = jnp.concatenate([flat, jnp.zeros((1, staged.shape[2] - owners * slots), jnp.int32)], axis=1)
    for n in range(staged.shape[0]):
        staged[n] = flat
    save = pltpu.make_async_copy(staged, message, sems.at[1])
    save.start()
    save.wait()
    load.wait()


def asked_at(asked, n, w, k):
    return jnp.maximum(asked[n, 0, (k % 2) * 32 + (k // 2) * 8 + w], 0)


def serve_kernel(asked, held, out):
    w = lax.axis_index("z2") * 4 + lax.axis_index("x")
    for n in range(out.shape[0]):
        for k in range(8):
            out[n, k] = held[(k // 2) * 8 + asked_at(asked, n, w, k)]


def three_parts(value):
    parts = []
    for _ in range(3):
        parts.append(value.astype(BF16).astype(F32))
        value = value - parts[-1]
    return parts


def geometry_kernel(atom, places, offset, xyz, phi, left_out, turned_out, inverse_far, inverse, spots, sems):
    batches, points = offset.shape[1], offset.shape[2]
    chunks = xyz.shape[1]
    ones = jnp.ones((1, points), F32)
    filler = jnp.zeros((128 - 24, points), F32)
    copies = []
    for b in range(batches):
        spot = [offset[k, b : b + 1] + places[k, atom[b]] for k in range(3)] + [ones]
        spot = jnp.concatenate(spot, axis=0)
        high, middle, low = three_parts(spot)
        stacked = jnp.concatenate([high, high, middle, high, low, middle, filler], axis=0)
        left_out[b] = stacked.T.astype(BF16)
        turned_out[b] = phi[b].T
        columns = jnp.concatenate([spot, jnp.zeros((124, points), F32)], axis=0).T
        for k in range(3):
            spots[k] = jnp.broadcast_to(columns[:, k : k + 1], (points, 128))

        def inverse_of(step, _, b=b):
            at = pl.ds(step * 64, 64)
            px, py, pz = (spots[k, at] for k in range(3))
            for h in range(chunks):
                gx = px - xyz[0, h : h + 1]
                gy = py - xyz[1, h : h + 1]
                gz = pz - xyz[2, h : h + 1]
                inverse[b, h, at] = lax.rsqrt(gx * gx + gy * gy + gz * gz + 1.0)
            return 0

        lax.fori_loop(0, points // 64, inverse_of, 0)
        copies.append(pltpu.make_async_copy(inverse.at[b], inverse_far.at[b], sems.at[b]))
        copies[-1].start()
    for copy in copies:
        copy.wait()


def density_kernel(needed, atom, phi, blocks, weight, offset, rho_out, rho_again, share_out, wide):
    batches, points, width = phi.shape
    rel = width // 128
    part = blocks.shape[2]
    lane = lax.broadcasted_iota(jnp.int32, (points, 128), 1)
    columns = jnp.zeros((points, 128), F32)
    for b in range(batches):
        for p in range(rel * rel):
            w, k = place_of(needed[b, p])
            i, j = p // rel, p % rel
            for c in range(2):
                for y2 in range(2):
                    at = i * 128 + (c * 2 + y2) * part
                    wide[b % 2, pl.ds(at, part), pl.ds(j * 128, 128)] = blocks[(y2 * 2 + c) * 8 + w, k]
        values = phi[b]
        product = jnp.dot(values, wide[b % 2], preferred_element_type=F32) * values.astype(F32)
        folded = product[:, :128]
        for j in range(1, rel):
            folded = folded + product[:, j * 128 : (j + 1) * 128]
        columns = jnp.where(lane == b, jnp.sum(folded, axis=1, keepdims=True), columns)
    rho = columns.T[:batches]
    rho_out[...] = rho
    rho_again[...] = rho
    weighted = rho * weight[...]
    moments = [weighted] + [weighted * offset[k] for k in range(3)]
    spot = lax.broadcasted_iota(jnp.int32, (batches, 128), 1)
    row = lax.broadcasted_iota(jnp.int32, (batches, 128), 0)
    tile = jnp.zeros((batches, 128), F32)
    for k, moment in enumerate(moments):
        tile = jnp.where(spot % VALUES == k, jnp.sum(moment, axis=1, keepdims=True), tile)
    for b in range(batches):
        mine = row == b
        tile = jnp.where((spot % VALUES == 4) & mine, (atom[b] & 127).astype(F32), tile)
        tile = jnp.where((spot % VALUES == 5) & mine, (atom[b] >> 7).astype(F32), tile)
    tile = jnp.where(spot // VALUES == row, tile, 0.0)
    flat = jnp.sum(tile, axis=0, keepdims=True)[:, : batches * VALUES]
    for n in range(share_out.shape[0]):
        share_out[n] = flat


def relay_kernel(near, out):
    row = jnp.concatenate([near[n] for n in range(near.shape[0])], axis=1)
    for n in range(out.shape[0]):
        out[n] = row


def term_kernel(
    needed,
    shares,
    rho,
    weight,
    exchange_part,
    xyz,
    left,
    turned_phi,
    phi,
    inverse_far,
    multipoles_out,
    out,
    inverse,
    rows,
    right,
    total,
    load_sems,
):
    batches, points, width = phi.shape
    loads = [pltpu.make_async_copy(inverse_far.at[b], inverse.at[b], load_sems.at[b]) for b in range(batches)]
    for load in loads:
        load.start()
    rel = width // 128
    devices = rows.shape[0]
    sources = shares.shape[0]
    each = batches * VALUES
    chunks = xyz.shape[1]
    atoms = multipoles_out.shape[1]

    rows[...] = jnp.zeros_like(rows)
    near = shares[...].reshape(sources, shares.shape[2])
    for g in range(devices // sources):
        rows[g * sources : (g + 1) * sources, :each] = near[:, g * each : (g + 1) * each]
    table = rows[...]
    turned = table.T
    low_at = lax.broadcasted_iota(jnp.int32, (devices, 128), 1).astype(F32)
    high_at = lax.broadcasted_iota(jnp.int32, (chunks, devices), 0).astype(F32)
    summed = jnp.zeros((12 * chunks, 128), F32)
    for b in range(batches):
        low = jnp.where(table[:, b * VALUES + 4 : b * VALUES + 5] == low_at, 1.0, 0.0).astype(BF16)
        high = jnp.where(turned[b * VALUES + 5 : b * VALUES + 6] == high_at, 1.0, 0.0)
        stacked = []
        for piece in three_parts(turned[b * VALUES : (b + 1) * VALUES]):
            stacked += [high * piece[k : k + 1] for k in range(4)]
        stacked = jnp.concatenate(stacked, axis=0).astype(BF16)
        summed = summed + jnp.dot(stacked, low, preferred_element_type=F32)
    multipoles = [
        summed[k * chunks : (k + 1) * chunks]
        + (summed[(4 + k) * chunks : (5 + k) * chunks] + summed[(8 + k) * chunks : (9 + k) * chunks])
        for k in range(4)
    ]
    for k in range(4):
        for h in range(chunks):
            count = min(128, atoms - h * 128)
            multipoles_out[k : k + 1, h * 128 : h * 128 + count] = multipoles[k][h : h + 1, :count]

    shift = multipoles[1] * xyz[0] + multipoles[2] * xyz[1] + multipoles[3] * xyz[2]
    parts = [three_parts(value) for value in (multipoles[1], multipoles[2], multipoles[3], -shift)]
    right[...] = jnp.zeros_like(right)
    for h in range(chunks):
        stacked = [parts[k][n][h : h + 1] for n in (0, 1, 0, 2, 0, 1) for k in range(4)]
        stacked = jnp.concatenate(stacked + [jnp.zeros((8, 128), F32)], axis=0)
        right[:32, h * 128 : (h + 1) * 128] = stacked.astype(BF16)

    total[...] = jnp.zeros_like(total)
    for b in range(batches):
        dipole = jnp.dot(left[b], right[...], preferred_element_type=F32)
        loads[b].wait()
        acc = jnp.zeros((points, 128), F32)
        for h in range(chunks):
            s = inverse[b, h]
            acc = acc + s * (multipoles[0][h : h + 1] + dipole[:, h * 128 : (h + 1) * 128] * (s * s))
        hartree = jnp.sum(acc.T, axis=0, keepdims=True)
        factor = weight[b : b + 1] * (exchange_part[b : b + 1] * rho[b : b + 1] + hartree)
        scaled = (turned_phi[b].astype(F32) * factor).astype(BF16)
        for i in range(rel):
            term = jnp.dot(scaled[i * 128 : (i + 1) * 128], phi[b], preferred_element_type=F32)
            for j in range(rel):
                q = needed[b, i * rel + j]
                total[q] += term[:, j * 128 : (j + 1) * 128]

    for w in range(8):
        for k in range(8):
            q = (k // 2) * 16 + w * 2 + k % 2
            for c in range(2):
                for y2 in range(2):
                    first = c * 64 + y2 * 32
                    out[(y2 * 2 + c) * 8 + w, k] = total[q, first : first + 32].astype(BF16)


def collect_kernel(asked, received, out, *totals):
    for total in totals:
        total[...] = jnp.zeros_like(total)
    w = lax.axis_index("z2") * 4 + lax.axis_index("x")

    def add_one(n, _):
        for k, total in enumerate(totals):
            total[asked_at(asked, n, w, k)] += received[n, k].astype(F32)
        return 0

    lax.fori_loop(0, received.shape[0], add_one, 0)
    for z4 in range(4):
        for h in range(4):
            two = [totals[2 * z4][2 * h + e] + totals[2 * z4 + 1][2 * h + e] for e in range(2)]
            for y4 in range(4):
                pair = jnp.concatenate([value[y4 * 8 : (y4 + 1) * 8] for value in two], axis=0)
                out[y4 * 4 + z4, h * 16 : (h + 1) * 16] = pair.astype(BF16)


def settle_kernel(received, out):
    summed = received[0].astype(F32)
    for n in range(1, received.shape[0]):
        summed = summed + received[n].astype(F32)
    summed = summed.astype(BF16)
    for n in range(out.shape[0]):
        out[n] = summed


def on_device(
    basis_values,
    stored_density_blocks,
    device_request,
    batch_blocks,
    batch_atom,
    point_offset,
    point_weight,
    exchange_kernel,
    atom_xyz,
):
    batches, points, width = basis_values.shape
    own, tile = stored_density_blocks.shape[0], stored_density_blocks.shape[1]
    atoms = atom_xyz.shape[1]
    padded = -(-atoms // 128) * 128
    part = tile // 4
    chunks = padded // 128
    each = batches * VALUES
    params = pltpu.CompilerParams(vmem_limit_bytes=32 * MIB)
    hbm = pl.BlockSpec(memory_space=pltpu.HBM)

    far = jnp.pad(atom_xyz, ((0, 0), (0, padded - atoms))).reshape(3, chunks, 128)
    left, turned_phi, inverse = pl.pallas_call(
        geometry_kernel,
        name="geometry",
        out_shape=(
            jax.ShapeDtypeStruct((batches, points, 128), BF16),
            jax.ShapeDtypeStruct((batches, width, points), BF16),
            pltpu.HBM((batches, chunks, points, 128), F32),
        ),
        in_specs=smem(2) + vmem(3),
        out_specs=tuple(vmem(2)) + (hbm,),
        scratch_shapes=[
            pltpu.VMEM((batches, chunks, points, 128), F32),
            pltpu.VMEM((3, points, 128), F32),
            pltpu.SemaphoreType.DMA((batches,)),
        ],
        compiler_params=params,
        cost_estimate=pl.CostEstimate(flops=2 * 10**7, bytes_accessed=6 * MIB, transcendentals=10**6),
    )(batch_atom, atom_xyz, point_offset, far, basis_values)

    message, slab = pl.pallas_call(
        prepare_kernel,
        name="prepare",
        out_shape=(pltpu.HBM((32, 1, 128), jnp.int32), jax.ShapeDtypeStruct((own, part, tile), BF16)),
        in_specs=[hbm, hbm],
        out_specs=(hbm, vmem(1)[0]),
        scratch_shapes=[
            pltpu.VMEM((1, 2, 32), jnp.int32),
            pltpu.VMEM((32, 1, 128), jnp.int32),
            pltpu.SemaphoreType.DMA((3,)),
        ],
        compiler_params=params,
    )(
        pltpu.with_memory_space_constraint(device_request.transpose(0, 2, 1), pltpu.HBM),
        pltpu.with_memory_space_constraint(stored_density_blocks, pltpu.HBM),
    )
    asked = exchange(message, COLLECT)
    pieces = lax.all_gather(slab, "z4", tiled=True)
    served = pl.pallas_call(
        serve_kernel,
        name="serve",
        out_shape=jax.ShapeDtypeStruct((32, 8, part, tile), BF16),
        in_specs=smem(1) + vmem(1),
        out_specs=vmem(1)[0],
        compiler_params=params,
    )(asked, pieces)
    blocks = exchange(served, COLLECT)

    density, density_again, share = pl.pallas_call(
        density_kernel,
        name="density",
        out_shape=(
            jax.ShapeDtypeStruct((batches, points), F32),
            jax.ShapeDtypeStruct((batches, points), F32),
            jax.ShapeDtypeStruct((8, 1, each), F32),
        ),
        in_specs=smem(2) + vmem(4),
        out_specs=tuple(vmem(3)),
        scratch_shapes=[pltpu.VMEM((2, width, width), BF16)],
        compiler_params=params,
    )(batch_blocks, batch_atom, basis_values, blocks, point_weight, point_offset)

    shares = pl.pallas_call(
        relay_kernel,
        name="relay",
        out_shape=jax.ShapeDtypeStruct((64, 1, 8 * each), F32),
        in_specs=vmem(1),
        out_specs=vmem(1)[0],
        compiler_params=params,
    )(exchange(share, NEAR))
    multipoles, outgoing = pl.pallas_call(
        term_kernel,
        name="terms",
        out_shape=(
            jax.ShapeDtypeStruct((4, atoms), F32),
            jax.ShapeDtypeStruct((32, 8, 32, tile), BF16),
        ),
        in_specs=smem(1) + vmem(8) + [hbm],
        out_specs=tuple(vmem(2)),
        scratch_shapes=[
            pltpu.VMEM(inverse.shape, F32),
            pltpu.VMEM((512, 128), F32),
            pltpu.VMEM((128, padded), BF16),
            pltpu.VMEM((64, tile, tile), F32),
            pltpu.SemaphoreType.DMA((batches,)),
        ],
        compiler_params=params,
    )(
        batch_blocks,
        exchange(shares, FAR),
        density_again,
        point_weight,
        exchange_kernel,
        far,
        left,
        turned_phi,
        basis_values,
        pltpu.with_memory_space_constraint(inverse, pltpu.HBM),
    )

    received = exchange(outgoing, COLLECT)
    partial = pl.pallas_call(
        collect_kernel,
        name="collect",
        out_shape=jax.ShapeDtypeStruct((16, own * 8, tile), BF16),
        in_specs=smem(1) + vmem(1),
        out_specs=vmem(1)[0],
        scratch_shapes=[pltpu.VMEM((own, 32, tile), F32)] * 8,
        compiler_params=params,
    )(asked, received)
    settled = pl.pallas_call(
        settle_kernel,
        name="settle",
        out_shape=jax.ShapeDtypeStruct((16, own * 8, tile), BF16),
        in_specs=vmem(1),
        out_specs=vmem(1)[0],
        compiler_params=params,
    )(exchange(partial, SETTLE))
    rows = exchange(settled, GRP)
    rows = rows.reshape(4, 2, 2, own, 8, tile).transpose(3, 2, 1, 0, 4, 5)
    return (rows.reshape(own, tile, tile), density, multipoles)


def solution(mesh):
    finer = Mesh(mesh.devices.reshape(4, 2, 2, 4, 2, 4), GRP_DEV)
    placed = (
        P(GRP_DEV, None, None),
        P(DEV, None, None),
        P(GRP_DEV, None, None),
        P(GRP_DEV, None),
        P(GRP_DEV),
        P(None, GRP_DEV, None),
        P(GRP_DEV, None),
        P(GRP_DEV, None),
        P(),
    )
    return jax.shard_map(
        on_device,
        mesh=finer,
        in_specs=placed,
        out_specs=(P(DEV, None, None), P(GRP_DEV, None), P()),
        check_vma=False,
    )
```

```python
import functools

import jax
import jax.numpy as jnp
from jax import lax
from jax.experimental import pallas as pl
from jax.experimental.pallas import tpu as pltpu
from jax.sharding import Mesh
from jax.sharding import PartitionSpec as P

GRP = ("y4", "y2", "c")
DEV = ("z4", "z2", "x")
GRP_DEV = GRP + DEV
COLLECT = ("y2", "c", "z2", "x")
SETTLE = ("y4", "z4")

F32 = jnp.float32
BF16 = jnp.bfloat16
MIB = 1024 * 1024
VALUES = 8


def exchange(value, axes):
    return lax.all_to_all(value, axes, split_axis=0, concat_axis=0, tiled=True)


def vmem(count):
    return [pl.BlockSpec(memory_space=pltpu.VMEM)] * count


def smem(count):
    return [pl.BlockSpec(memory_space=pltpu.SMEM)] * count


def place_of(position):
    return (position >> 1) & 7, (position >> 4) * 2 + (position & 1)


def prepare_kernel(request_far, stored, message, slab, request, staged, sems):
    ask = pltpu.make_async_copy(request_far, request, sems.at[2])
    ask.start()
    part = slab.shape[1]
    at = (lax.axis_index("c") * 2 + lax.axis_index("y2")) * part
    own = stored.at[:, pl.ds(pl.multiple_of(at, part), part)]
    load = pltpu.make_async_copy(own, slab, sems.at[0])
    load.start()
    slots, owners = request.shape[1], request.shape[2]
    ask.wait()
    flat = jnp.concatenate([request[0, k : k + 1] for k in range(slots)], axis=1)
    flat = jnp.concatenate([flat, jnp.zeros((1, staged.shape[2] - owners * slots), jnp.int32)], axis=1)
    for n in range(staged.shape[0]):
        staged[n] = flat
    save = pltpu.make_async_copy(staged, message, sems.at[1])
    save.start()
    save.wait()
    load.wait()


def asked_at(asked, n, w, k):
    return jnp.maximum(asked[n, 0, (k % 2) * 32 + (k // 2) * 8 + w], 0)


def serve_kernel(asked, held, out):
    w = lax.axis_index("z2") * 4 + lax.axis_index("x")
    for n in range(out.shape[0]):
        for k in range(8):
            out[n, k] = held[(k // 2) * 8 + asked_at(asked, n, w, k)]


def three_parts(value):
    parts = []
    for _ in range(3):
        parts.append(value.astype(BF16).astype(F32))
        value = value - parts[-1]
    return parts


def geometry_kernel(atom, places, offset, xyz, phi, left_out, turned_out, inverse_far, inverse, spots, sems):
    batches, points = offset.shape[1], offset.shape[2]
    chunks = xyz.shape[1]
    ones = jnp.ones((1, points), F32)
    filler = jnp.zeros((128 - 24, points), F32)
    copies = []
    for b in range(batches):
        spot = [offset[k, b : b + 1] + places[k, atom[b]] for k in range(3)] + [ones]
        spot = jnp.concatenate(spot, axis=0)
        high, middle, low = three_parts(spot)
        stacked = jnp.concatenate([high, high, middle, high, low, middle, filler], axis=0)
        left_out[b] = stacked.T.astype(BF16)
        turned_out[b] = phi[b].T
        columns = jnp.concatenate([spot, jnp.zeros((124, points), F32)], axis=0).T
        for k in range(3):
            spots[k] = jnp.broadcast_to(columns[:, k : k + 1], (points, 128))

        def inverse_of(step, _, b=b):
            at = pl.ds(step * 64, 64)
            px, py, pz = (spots[k, at] for k in range(3))
            for h in range(chunks):
                gx = px - xyz[0, h : h + 1]
                gy = py - xyz[1, h : h + 1]
                gz = pz - xyz[2, h : h + 1]
                inverse[b, h, at] = lax.rsqrt(gx * gx + gy * gy + gz * gz + 1.0)
            return 0

        lax.fori_loop(0, points // 64, inverse_of, 0)
        copies.append(pltpu.make_async_copy(inverse.at[b], inverse_far.at[b], sems.at[b]))
        copies[-1].start()
    for copy in copies:
        copy.wait()


def density_kernel(needed, atom, phi, blocks, weight, offset, rho_out, rho_again, share_out, wide):
    batches, points, width = phi.shape
    rel = width // 128
    part = blocks.shape[2]
    lane = lax.broadcasted_iota(jnp.int32, (points, 128), 1)
    columns = jnp.zeros((points, 128), F32)
    for b in range(batches):
        for p in range(rel * rel):
            w, k = place_of(needed[b, p])
            i, j = p // rel, p % rel
            for c in range(2):
                for y2 in range(2):
                    at = i * 128 + (c * 2 + y2) * part
                    wide[b % 2, pl.ds(at, part), pl.ds(j * 128, 128)] = blocks[(y2 * 2 + c) * 8 + w, k]
        values = phi[b]
        product = jnp.dot(values, wide[b % 2], preferred_element_type=F32) * values.astype(F32)
        folded = product[:, :128]
        for j in range(1, rel):
            folded = folded + product[:, j * 128 : (j + 1) * 128]
        columns = jnp.where(lane == b, jnp.sum(folded, axis=1, keepdims=True), columns)
    rho = columns.T[:batches]
    rho_out[...] = rho
    rho_again[...] = rho
    weighted = rho * weight[...]
    moments = [weighted] + [weighted * offset[k] for k in range(3)]
    spot = lax.broadcasted_iota(jnp.int32, (batches, 128), 1)
    row = lax.broadcasted_iota(jnp.int32, (batches, 128), 0)
    tile = jnp.zeros((batches, 128), F32)
    for k, moment in enumerate(moments):
        tile = jnp.where(spot % VALUES == k, jnp.sum(moment, axis=1, keepdims=True), tile)
    for b in range(batches):
        mine = row == b
        tile = jnp.where((spot % VALUES == 4) & mine, (atom[b] & 127).astype(F32), tile)
        tile = jnp.where((spot % VALUES == 5) & mine, (atom[b] >> 7).astype(F32), tile)
    tile = jnp.where(spot // VALUES == row, tile, 0.0)
    flat = jnp.sum(tile, axis=0, keepdims=True)[:, : batches * VALUES]
    for n in range(share_out.shape[0]):
        share_out[n] = flat


def relay_kernel(near, out):
    row = jnp.concatenate([near[n] for n in range(near.shape[0])], axis=1)
    for n in range(out.shape[0]):
        out[n] = row


def term_kernel(
    needed,
    shares,
    rho,
    weight,
    exchange_part,
    xyz,
    left,
    turned_phi,
    phi,
    inverse_far,
    multipoles_out,
    out,
    inverse,
    rows,
    right,
    total,
    load_sems,
):
    batches, points, width = phi.shape
    loads = [pltpu.make_async_copy(inverse_far.at[b], inverse.at[b], load_sems.at[b]) for b in range(batches)]
    for load in loads:
        load.start()
    rel = width // 128
    devices = rows.shape[0]
    sources = shares.shape[0]
    each = batches * VALUES
    chunks = xyz.shape[1]
    atoms = multipoles_out.shape[1]

    rows[...] = jnp.zeros_like(rows)
    near = shares[...].reshape(sources, shares.shape[2])
    for g in range(devices // sources):
        rows[g * sources : (g + 1) * sources, :each] = near[:, g * each : (g + 1) * each]
    table = rows[...]
    turned = table.T
    low_at = lax.broadcasted_iota(jnp.int32, (devices, 128), 1).astype(F32)
    high_at = lax.broadcasted_iota(jnp.int32, (chunks, devices), 0).astype(F32)
    summed = jnp.zeros((12 * chunks, 128), F32)
    for b in range(batches):
        low = jnp.where(table[:, b * VALUES + 4 : b * VALUES + 5] == low_at, 1.0, 0.0).astype(BF16)
        high = jnp.where(turned[b * VALUES + 5 : b * VALUES + 6] == high_at, 1.0, 0.0)
        stacked = []
        for piece in three_parts(turned[b * VALUES : (b + 1) * VALUES]):
            stacked += [high * piece[k : k + 1] for k in range(4)]
        stacked = jnp.concatenate(stacked, axis=0).astype(BF16)
        summed = summed + jnp.dot(stacked, low, preferred_element_type=F32)
    multipoles = [
        summed[k * chunks : (k + 1) * chunks]
        + (summed[(4 + k) * chunks : (5 + k) * chunks] + summed[(8 + k) * chunks : (9 + k) * chunks])
        for k in range(4)
    ]
    for k in range(4):
        for h in range(chunks):
            count = min(128, atoms - h * 128)
            multipoles_out[k : k + 1, h * 128 : h * 128 + count] = multipoles[k][h : h + 1, :count]

    shift = multipoles[1] * xyz[0] + multipoles[2] * xyz[1] + multipoles[3] * xyz[2]
    parts = [three_parts(value) for value in (multipoles[1], multipoles[2], multipoles[3], -shift)]
    right[...] = jnp.zeros_like(right)
    for h in range(chunks):
        stacked = [parts[k][n][h : h + 1] for n in (0, 1, 0, 2, 0, 1) for k in range(4)]
        stacked = jnp.concatenate(stacked + [jnp.zeros((8, 128), F32)], axis=0)
        right[:32, h * 128 : (h + 1) * 128] = stacked.astype(BF16)

    total[...] = jnp.zeros_like(total)
    for b in range(batches):
        dipole = jnp.dot(left[b], right[...], preferred_element_type=F32)
        loads[b].wait()
        acc = jnp.zeros((points, 128), F32)
        for h in range(chunks):
            s = inverse[b, h]
            acc = acc + s * (multipoles[0][h : h + 1] + dipole[:, h * 128 : (h + 1) * 128] * (s * s))
        hartree = jnp.sum(acc.T, axis=0, keepdims=True)
        factor = weight[b : b + 1] * (exchange_part[b : b + 1] * rho[b : b + 1] + hartree)
        scaled = (turned_phi[b].astype(F32) * factor).astype(BF16)
        for i in range(rel):
            term = jnp.dot(scaled[i * 128 : (i + 1) * 128], phi[b], preferred_element_type=F32)
            for j in range(rel):
                q = needed[b, i * rel + j]
                total[q] += term[:, j * 128 : (j + 1) * 128]

    for w in range(8):
        for k in range(8):
            q = (k // 2) * 16 + w * 2 + k % 2
            for c in range(2):
                for y2 in range(2):
                    first = c * 64 + y2 * 32
                    out[(y2 * 2 + c) * 8 + w, k] = total[q, first : first + 32].astype(BF16)


def collect_kernel(asked, received, out, *totals):
    for total in totals:
        total[...] = jnp.zeros_like(total)
    w = lax.axis_index("z2") * 4 + lax.axis_index("x")

    def add_one(n, _):
        for k, total in enumerate(totals):
            total[asked_at(asked, n, w, k)] += received[n, k].astype(F32)
        return 0

    lax.fori_loop(0, received.shape[0], add_one, 0, unroll=4)
    for z4 in range(4):
        for h in range(4):
            two = [totals[2 * z4][2 * h + e] + totals[2 * z4 + 1][2 * h + e] for e in range(2)]
            for y4 in range(4):
                pair = jnp.concatenate([value[y4 * 8 : (y4 + 1) * 8] for value in two], axis=0)
                out[y4 * 4 + z4, h * 16 : (h + 1) * 16] = pair.astype(BF16)


def settle_kernel(received, out):
    summed = received[0].astype(F32)
    for n in range(1, received.shape[0]):
        summed = summed + received[n].astype(F32)
    summed = summed.astype(BF16)
    for n in range(out.shape[0]):
        out[n] = summed


def on_device(
    basis_values,
    stored_density_blocks,
    device_request,
    batch_blocks,
    batch_atom,
    point_offset,
    point_weight,
    exchange_kernel,
    atom_xyz,
):
    batches, points, width = basis_values.shape
    own, tile = stored_density_blocks.shape[0], stored_density_blocks.shape[1]
    atoms = atom_xyz.shape[1]
    padded = -(-atoms // 128) * 128
    part = tile // 4
    chunks = padded // 128
    each = batches * VALUES
    params = pltpu.CompilerParams(vmem_limit_bytes=32 * MIB)
    hbm = pl.BlockSpec(memory_space=pltpu.HBM)

    far = jnp.pad(atom_xyz, ((0, 0), (0, padded - atoms))).reshape(3, chunks, 128)
    left, turned_phi, inverse = pl.pallas_call(
        geometry_kernel,
        name="geometry",
        out_shape=(
            jax.ShapeDtypeStruct((batches, points, 128), BF16),
            jax.ShapeDtypeStruct((batches, width, points), BF16),
            pltpu.HBM((batches, chunks, points, 128), F32),
        ),
        in_specs=smem(2) + vmem(3),
        out_specs=tuple(vmem(2)) + (hbm,),
        scratch_shapes=[
            pltpu.VMEM((batches, chunks, points, 128), F32),
            pltpu.VMEM((3, points, 128), F32),
            pltpu.SemaphoreType.DMA((batches,)),
        ],
        compiler_params=params,
        cost_estimate=pl.CostEstimate(flops=2 * 10**7, bytes_accessed=6 * MIB, transcendentals=10**6),
    )(batch_atom, atom_xyz, point_offset, far, basis_values)

    message, slab = pl.pallas_call(
        prepare_kernel,
        name="prepare",
        out_shape=(pltpu.HBM((32, 1, 128), jnp.int32), jax.ShapeDtypeStruct((own, part, tile), BF16)),
        in_specs=[hbm, hbm],
        out_specs=(hbm, vmem(1)[0]),
        scratch_shapes=[
            pltpu.VMEM((1, 2, 32), jnp.int32),
            pltpu.VMEM((32, 1, 128), jnp.int32),
            pltpu.SemaphoreType.DMA((3,)),
        ],
        compiler_params=params,
    )(
        pltpu.with_memory_space_constraint(device_request.transpose(0, 2, 1), pltpu.HBM),
        pltpu.with_memory_space_constraint(stored_density_blocks, pltpu.HBM),
    )
    asked = exchange(message, COLLECT)
    pieces = lax.all_gather(slab, "z4", tiled=True)
    served = pl.pallas_call(
        serve_kernel,
        name="serve",
        out_shape=jax.ShapeDtypeStruct((32, 8, part, tile), BF16),
        in_specs=smem(1) + vmem(1),
        out_specs=vmem(1)[0],
        compiler_params=params,
    )(asked, pieces)
    blocks = exchange(served, COLLECT)

    density, density_again, share = pl.pallas_call(
        density_kernel,
        name="density",
        out_shape=(
            jax.ShapeDtypeStruct((batches, points), F32),
            jax.ShapeDtypeStruct((batches, points), F32),
            jax.ShapeDtypeStruct((16, 1, each), F32),
        ),
        in_specs=smem(2) + vmem(4),
        out_specs=tuple(vmem(3)),
        scratch_shapes=[pltpu.VMEM((2, width, width), BF16)],
        compiler_params=params,
    )(batch_blocks, batch_atom, basis_values, blocks, point_weight, point_offset)

    shares = pl.pallas_call(
        relay_kernel,
        name="relay",
        out_shape=jax.ShapeDtypeStruct((32, 1, 16 * each), F32),
        in_specs=vmem(1),
        out_specs=vmem(1)[0],
        compiler_params=params,
    )(exchange(share, GRP))
    multipoles, outgoing = pl.pallas_call(
        term_kernel,
        name="terms",
        out_shape=(
            jax.ShapeDtypeStruct((4, atoms), F32),
            jax.ShapeDtypeStruct((32, 8, 32, tile), BF16),
        ),
        in_specs=smem(1) + vmem(8) + [hbm],
        out_specs=tuple(vmem(2)),
        scratch_shapes=[
            pltpu.VMEM(inverse.shape, F32),
            pltpu.VMEM((512, 128), F32),
            pltpu.VMEM((128, padded), BF16),
            pltpu.VMEM((64, tile, tile), F32),
            pltpu.SemaphoreType.DMA((batches,)),
        ],
        compiler_params=params,
    )(
        batch_blocks,
        exchange(shares, DEV),
        density_again,
        point_weight,
        exchange_kernel,
        far,
        left,
        turned_phi,
        basis_values,
        pltpu.with_memory_space_constraint(inverse, pltpu.HBM),
    )

    received = exchange(outgoing, COLLECT)
    partial = pl.pallas_call(
        collect_kernel,
        name="collect",
        out_shape=jax.ShapeDtypeStruct((16, own * 8, tile), BF16),
        in_specs=smem(1) + vmem(1),
        out_specs=vmem(1)[0],
        scratch_shapes=[pltpu.VMEM((own, 32, tile), F32)] * 8,
        compiler_params=params,
    )(asked, received)
    settled = pl.pallas_call(
        settle_kernel,
        name="settle",
        out_shape=jax.ShapeDtypeStruct((16, own * 8, tile), BF16),
        in_specs=vmem(1),
        out_specs=vmem(1)[0],
        compiler_params=params,
    )(exchange(partial, SETTLE))
    rows = exchange(settled, GRP)
    rows = rows.reshape(4, 2, 2, own, 8, tile).transpose(3, 2, 1, 0, 4, 5)
    return (rows.reshape(own, tile, tile), density, multipoles)


def solution(mesh):
    finer = Mesh(mesh.devices.reshape(4, 2, 2, 4, 2, 4), GRP_DEV)
    placed = (
        P(GRP_DEV, None, None),
        P(DEV, None, None),
        P(GRP_DEV, None, None),
        P(GRP_DEV, None),
        P(GRP_DEV),
        P(None, GRP_DEV, None),
        P(GRP_DEV, None),
        P(GRP_DEV, None),
        P(),
    )
    return jax.shard_map(
        on_device,
        mesh=finer,
        in_specs=placed,
        out_specs=(P(DEV, None, None), P(GRP_DEV, None), P()),
        check_vma=False,
    )
```
